128 devices in a mesh: lat: 16 (over x, z), dep: 8 (over y, core).
Axes of the slice: x: 4, y: 4, z: 4, core: 2. Of those that a mesh axis runs over, the one named last changes fastest.
Arguments:
- state: float32 [64, 64, 128], P('lat', 'dep'), may hold values from 0.2 to 1
- kappa: float32 [64, 64, 128], P('lat', 'dep'), may hold values from 0.3 to 3
- rate: float32 [64, 64], P('lat', 'dep'), may hold values from 1 to 4
- grads: float32 [3, 64, 64], replicated, may hold values from -0.75 to 0.75
- lift: float32 [4, 32, 128], replicated, may hold values from -0.375 to 0.375
- rhs: float32 [64, 64, 32, 128], P('lat', 'dep'), may hold values from -18 to 18
Outputs:
- update: float32 [64, 64, 32, 128], P('lat', 'dep')
The draws below stay inside these ranges and needn't reach their ends.
All inputs are finite; a program needn't handle non-finite values.
Results may differ from the reference program's by a relative error of at most 0.0003.
Values sent between devices are 32-bit elements; how exact they have to be, the bound alone decides.
A program may use at most 128 MiB of HBM per device.

```python
import math
import jax
import jax.numpy as jnp
from jax import lax

NODES = 64
NV = 32
KRY = 8
NXE = 64
NZE = 64


def draw_rhs(key, part):
    full_shape = (NXE, NZE, NV, 128)
    along_x = jnp.arange(NXE, dtype=jnp.float32) / max(NXE - 1, 1)
    along_z = jnp.arange(NZE, dtype=jnp.float32) / max(NZE - 1, 1)
    row_scale = 1.0 + along_x[:, None, None, None] + along_z[None, :, None, None]
    values = jnp.clip(jax.random.normal(key, full_shape, jnp.float32), -6.0, 6.0)
    return values * row_scale


def steps_of(own_key, shape, split, low, top_value):
    def one(position, blocks):
        heights = jax.random.uniform(jax.random.fold_in(jax.random.fold_in(own_key, 6), position), (blocks,), jnp.float32, low / len(split), top_value / len(split))
        return jnp.repeat(jnp.exp(heights), shape[position] // blocks).reshape((-1,) + (1,) * (len(shape) - position - 1))

    loudness = one(*split[0])
    for cut in split[1:]:
        loudness = loudness * one(*cut)
    return loudness


def centred(own_key, dims, scale, bound, kind=jnp.bfloat16):
    return jnp.clip(scale * jax.random.normal(own_key, dims, jnp.float32), -bound, bound).astype(kind)


def setup_inputs(seed: int = 0) -> dict:
    key_list = jax.random.split(jax.random.key(seed), 7)
    return {
        "state": jnp.clip(0.2 + 0.8 * jax.random.uniform(key_list[0], (NXE, NZE, 128), jnp.float32) ** steps_of(key_list[0], (NXE, NZE, 128), ((0, 16), (1, 8)), -0.2, 0.2), 0.2, 1.0),
        "kappa": jnp.clip(jnp.exp(math.log(3.0) - 2.3025851 * jax.random.uniform(key_list[1], (NXE, NZE, 128), jnp.float32) ** steps_of(key_list[1], (NXE, NZE, 128), ((0, 16), (1, 8)), -0.2, 0.2)), 0.3, 3.0),
        "rate": jnp.clip(jnp.exp(math.log(4.0) - 1.3862944 * jax.random.uniform(key_list[2], (NXE, NZE), jnp.float32) ** steps_of(key_list[2], (NXE, NZE), ((0, 16), (1, 8)), -0.2, 0.2)), 1.0, 4.0),
        "grads": centred(key_list[3], (3, NODES, NODES), NODES ** -0.5, 0.75, jnp.float32),
        "lift": centred(key_list[4], (4, 32, 128), 256 ** -0.5, 0.375, jnp.float32),
        "rhs": draw_rhs(jax.random.fold_in(key_list[6], 71), 0),
    }


highest = lax.Precision.HIGHEST
mass_shift = 0.25

def face_table():
    unknown = jnp.arange(128, dtype=jnp.int32)[:, None]
    column = jnp.arange(128, dtype=jnp.int32)[None, :]
    face_id = column // 32
    species = column // 16 % 2
    along_one = column % 16 // 4
    along_two = column % 4
    edge_pos = 3 * (face_id % 2)
    is_lateral = face_id < 2
    node_x = jnp.where(is_lateral, edge_pos, along_one)
    node_y = jnp.where(is_lateral, along_one, along_two)
    node_z = jnp.where(is_lateral, along_two, edge_pos)
    target = species * 64 + node_x * 16 + node_y * 4 + node_z
    return (unknown == target).astype(jnp.float32)

def pairing_table():
    unknown = jnp.arange(128, dtype=jnp.int32)
    return (unknown[:, None] % 64 == unknown[None, :] % 64).astype(jnp.float32)

def element_tiles(kappa_rows, state_rows, rate_rows, grads, select):
    row_count = kappa_rows.shape[0]
    split_kappa = kappa_rows.reshape(row_count, 2, 64)
    stiffness = jnp.einsum('dqi,nsq,dqj->nsij', grads, split_kappa, grads, precision=highest)
    zero_block = jnp.zeros((row_count, 64, 64), jnp.float32)
    top_half = jnp.concatenate([stiffness[:, 0], zero_block], axis=2)
    bottom_half = jnp.concatenate([zero_block, stiffness[:, 1]], axis=2)
    face_kappa = jnp.dot(kappa_rows, select, precision=highest)
    penalty = jnp.dot(face_kappa, select.T, precision=highest)
    partner = jnp.concatenate([state_rows[:, 64:], state_rows[:, :64]], axis=1)
    identity = jnp.eye(128, dtype=jnp.float32)
    diag_tiles = jnp.concatenate([top_half, bottom_half], axis=1)
    diag_tiles = diag_tiles + identity[None] * (mass_shift + penalty)[:, None, :]
    diag_tiles = diag_tiles + pairing_table()[None] * (rate_rows[:, None] * partner)[:, None, :]
    return (diag_tiles, face_kappa)

def apply_operator(vectors, diag_tiles, weight, lift_cat, select):
    traces = jnp.einsum('xzvu,uk->xzvk', vectors, select, precision=highest)
    zero_row = jnp.zeros_like(traces[:, :1, :, :32])
    from_left = jnp.roll(traces[..., 32:64], 1, axis=0)
    from_right = jnp.roll(traces[..., 0:32], -1, axis=0)
    from_below = jnp.concatenate([zero_row, traces[:, :-1, :, 96:128]], axis=1)
    from_above = jnp.concatenate([traces[:, 1:, :, 64:96], zero_row], axis=1)
    near_traces = jnp.concatenate([from_left, from_right, from_below, from_above], axis=-1)
    own_part = jnp.einsum('xzij,xzvj->xzvi', diag_tiles, vectors, precision=highest)
    coupled = jnp.einsum('xzvk,ki->xzvi', near_traces * weight[:, :, None, :], lift_cat, precision=highest)
    return own_part - coupled

def inner_global(left_block, right_block):
    return jnp.einsum('xzvu,xzwu->vw', left_block, right_block, precision=highest)

def combine_columns(vectors, matrix):
    return jnp.einsum('xzvu,vw->xzwu', vectors, matrix, precision=highest)

def factor(gram_matrix):
    lower_factor = jnp.linalg.cholesky(gram_matrix)
    identity = jnp.eye(gram_matrix.shape[0], dtype=gram_matrix.dtype)
    inverse = jax.scipy.linalg.solve_triangular(lower_factor, identity, lower=True)
    return (lower_factor.T, inverse.T)

def reference(state, kappa, rate, grads, lift, rhs):
    select = face_table()

    def one_row(row_data):
        return element_tiles(row_data[0], row_data[1], row_data[2], grads, select)
    diag_tiles, face_kappa = lax.map(one_row, (kappa, state, rate))
    zero_col = jnp.zeros_like(face_kappa[:, :1, :32])
    weight = jnp.concatenate([jnp.roll(face_kappa[..., 32:64], 1, axis=0), face_kappa[..., 32:64], jnp.concatenate([zero_col, face_kappa[:, :-1, 96:128]], axis=1), face_kappa[..., 96:128]], axis=-1)
    lift_cat = jnp.concatenate([lift[0], lift[1], lift[2], lift[3]], axis=0)
    columns = rhs.shape[2]
    start_factor, inverse = factor(inner_global(rhs, rhs))
    basis_list = [combine_columns(rhs, inverse)]
    coef_table = []
    for step_index in range(KRY):
        image_block = apply_operator(basis_list[step_index], diag_tiles, weight, lift_cat, select)
        column_coefs = []
        for prior in range(step_index + 1):
            column_coefs.append(inner_global(basis_list[prior], image_block))
        for prior in range(step_index + 1):
            image_block = image_block - combine_columns(basis_list[prior], column_coefs[prior])
        upper_factor, inverse = factor(inner_global(image_block, image_block))
        column_coefs.append(upper_factor)
        coef_table.append(column_coefs)
        basis_list.append(combine_columns(image_block, inverse))
    zero_small = jnp.zeros((columns, columns), jnp.float32)
    block_rows = []
    for row_index in range(KRY + 1):
        row_blocks = []
        for col_index in range(KRY):
            if row_index <= col_index + 1:
                row_blocks.append(coef_table[col_index][row_index])
            else:
                row_blocks.append(zero_small)
        block_rows.append(jnp.concatenate(row_blocks, axis=1))
    hessenberg = jnp.concatenate(block_rows, axis=0)
    gram_small = jnp.dot(hessenberg.T, hessenberg, precision=highest)
    right_side = jnp.dot(hessenberg[:columns].T, start_factor, precision=highest)
    coeffs = jax.scipy.linalg.cho_solve((jnp.linalg.cholesky(gram_small), True), right_side)
    update = combine_columns(basis_list[0], coeffs[:columns])
    for step_index in range(1, KRY):
        update = update + combine_columns(basis_list[step_index], coeffs[step_index * columns:(step_index + 1) * columns])
    return update
```

```python
import functools

import jax
import jax.numpy as jnp
from jax import lax
from jax.experimental import pallas as pl
from jax.experimental.pallas import tpu as pltpu
from jax.sharding import PartitionSpec as P

MESH = pl.DeviceIdType.MESH
highest = lax.Precision.HIGHEST
f32 = jnp.float32
bf16 = jnp.bfloat16

A_ROWS, E_ROWS = 4, 8
ELEMS = A_ROWS * E_ROWS
NV = 32
LANES = (128, 256, 256, 384)
ROWS = (128, 64, 64, 64)

NN = (((1,), (0,)), ((), ()))
NT = (((1,), (1,)), ((), ()))


def split(x):
    hi = x.astype(bf16)
    return hi, (x - hi.astype(f32)).astype(bf16)


def dot(a, b, dims=NN):
    return lax.dot_general(a, b, dims, preferred_element_type=f32)


def dot_exact(a, b, dims=NN):
    return lax.dot_general(a, b, dims, precision=highest, preferred_element_type=f32)


def dot3(ah, al, bh, bl, dims=NN):
    rows = ah.shape[0]
    both = dot(jnp.concatenate([ah, al], axis=0), bh, dims)
    return both[:rows] + both[rows:] + dot(ah, bl, dims)


def iota(shape, dim):
    return lax.broadcasted_iota(jnp.int32, shape, dim)


def eye(n):
    return (iota((n, n), 0) == iota((n, n), 1)).astype(f32)


def eliminate(gram):
    n = gram.shape[0]
    wide = jnp.concatenate([gram, eye(n)], axis=1)
    width = 2 * n
    row = iota((n, width), 0)
    for k in range(n - 1):
        column = jnp.broadcast_to(wide[:, k : k + 1], (n, width))
        pivot = column[k : k + 1, :]
        scaled = wide[k : k + 1, :] * (1.0 / pivot)
        wide = wide - jnp.where(row > k, column, 0.0) * scaled
    diag = jnp.sum(jnp.where(row == iota((n, width), 1), wide, 0.0), axis=1, keepdims=True)
    wide = wide * lax.rsqrt(diag)
    upper = jnp.where(iota((n, n), 0) <= iota((n, n), 1), wide[:, :n], 0.0)
    return upper, wide[:, n:]


def kernel(
    n_lat,
    n_dep,
    kappa_ref,
    state_ref,
    rate_ref,
    gt_ref,
    ga_ref,
    gb_ref,
    m_ref,
    rhs_ref,
    out_ref,
    basis_hi,
    basis_lo,
    stiff_hi,
    stiff_lo,
    field_a,
    field_b,
    own,
    kappa_pad,
    kappa_x,
    kappa_z,
    diag,
    cross,
    m_hi,
    m_lo,
    halo_out,
    halo_in,
    hess,
    nfac,
    ninv,
    ysol,
    sums,
    take_a,
    part,
    take_b,
    total,
    halo_send,
    halo_recv,
    a_send,
    a_recv,
    b_send,
    b_recv,
    c_send,
    c_recv,
):
    lat = lax.axis_index("lat")
    dep = lax.axis_index("dep")

    barrier = pltpu.get_barrier_semaphore()
    for k in range(1, n_dep):
        pl.semaphore_signal(
            barrier, inc=1, device_id=(lat, lax.rem(dep + k, n_dep)), device_id_type=MESH
        )
    for k in range(1, n_lat):
        pl.semaphore_signal(
            barrier, inc=1, device_id=(lax.rem(lat + k, n_lat), dep), device_id_type=MESH
        )

    lane = iota((1, 128), 1)
    node_x = lane % 64 // 16
    node_z = lane % 4

    kappa = kappa_ref[...]
    lanes32 = iota((ELEMS, 128), 1)
    edge_x = (lanes32 % 64 // 16 == 0) | (lanes32 % 64 // 16 == 3)
    edge_z = (lanes32 % 4 == 0) | (lanes32 % 4 == 3)
    touches = edge_x.astype(f32) + edge_z.astype(f32)
    diag[...] = 0.25 + kappa * touches
    cross[...] = rate_ref[...] * pltpu.roll(state_ref[...], 64, 1)
    kappa_x[...] = pltpu.roll(kappa, 80, 1)
    kappa_z[...] = pltpu.roll(kappa, 125, 1)
    kappa_pad[...] = jnp.ones_like(kappa_pad)
    for a in range(A_ROWS):
        base = (a + 1) * 10 + 1
        kappa_pad[base : base + E_ROWS, :] = kappa[a * E_ROWS : (a + 1) * E_ROWS, :]
    mh, ml = split(m_ref[...])
    m_hi[...] = mh
    m_lo[...] = ml
    for k in range(A_ROWS):
        for side in (0, E_ROWS + 1):
            field_a[(k + 1) * 10 + side] = jnp.zeros((NV, 128), f32)
            field_b[(k + 1) * 10 + side] = jnp.zeros((NV, 128), f32)

    def padded(el):
        return (el // E_ROWS + 1) * 10 + el % E_ROWS + 1

    @pl.loop(0, ELEMS)
    def _(el):
        row = kappa_ref[pl.ds(el, 1), :]
        turned = pltpu.roll(row, 64, 1)
        first = jnp.where(lane < 64, row, turned)
        second = jnp.where(lane < 64, turned, row)
        first = jnp.concatenate([first, first], axis=1)
        second = jnp.concatenate([second, second], axis=1)
        upper = dot_exact(gt_ref[...] * first, ga_ref[...])
        lower = dot_exact(gt_ref[...] * second, gb_ref[...])
        sh, sl = split(jnp.concatenate([upper, lower], axis=0))
        stiff_hi[el] = sh
        stiff_lo[el] = sl
        v = rhs_ref[el]
        vh, vl = split(v)
        basis_hi[el, 0:NV, :] = vh
        basis_lo[el, 0:NV, :] = vl
        field_a[padded(el)] = v

    pl.semaphore_wait(barrier, n_lat + n_dep - 2)

    def halo_copies(slot):
        right, left = lax.rem(lat + 1, n_lat), lax.rem(lat + n_lat - 1, n_lat)
        copies = []
        for index, (start, size, where) in enumerate(
            (
                (0, 2, (right, dep)),
                (2, 2, (left, dep)),
                (4, 1, (lat, lax.rem(dep + 1, n_dep))),
                (5, 1, (lat, lax.rem(dep + n_dep - 1, n_dep))),
            )
        ):
            copies.append(
                pltpu.make_async_remote_copy(
                    src_ref=halo_out.at[slot, pl.ds(start, size)],
                    dst_ref=halo_in.at[slot, pl.ds(start, size)],
                    send_sem=halo_send.at[slot, index],
                    recv_sem=halo_recv.at[slot, index],
                    device_id=where,
                    device_id_type=MESH,
                )
            )
        return copies

    has_above = dep < n_dep - 1
    has_below = dep > 0

    def operator(field, field_out, slot_in, slot_out, shift, parity):
        for p in range(2):
            right = None
            left = None
            for k in range(4):
                e = 4 * p + k
                index = 4 * 10 + e + 1
                there = pltpu.roll(
                    field[index] * kappa_pad[index : index + 1, :], (80 + 16 * k) % 128, 1
                )
                back = pltpu.roll(field[10 + e + 1], 16 * k, 1)
                mask = node_x == k
                right = there if right is None else jnp.where(mask, there, right)
                left = back if left is None else jnp.where(mask, back, left)
            halo_out[parity, p] = right
            halo_out[parity, 2 + p] = left
        up = None
        down = None
        for k in range(A_ROWS):
            index = (k + 1) * 10 + E_ROWS
            there = pltpu.roll(
                field[index] * kappa_pad[index : index + 1, :], (125 + k) % 128, 1
            )
            back = pltpu.roll(field[(k + 1) * 10 + 1], k, 1)
            mask = node_z == k
            up = there if up is None else jnp.where(mask, there, up)
            down = back if down is None else jnp.where(mask, back, down)
        halo_out[parity, 4] = up
        halo_out[parity, 5] = down
        copies = halo_copies(parity)
        copies[0].start()
        copies[1].start()

        @pl.when(has_above)
        def _():
            copies[2].start()

        @pl.when(has_below)
        def _():
            copies[3].start()

        @pl.loop(0, ELEMS // 2)
        def _(pair):
            for half in range(2):
                el = pair * 2 + half
                xh = basis_hi[el, slot_in * NV : (slot_in + 1) * NV, :]
                xl = basis_lo[el, slot_in * NV : (slot_in + 1) * NV, :]
                x = field[padded(el)]
                z = x * cross[pl.ds(el, 1), :]
                y = dot3(xh, xl, stiff_hi[el], stiff_lo[el])
                here = diag[pl.ds(el, 1), :]
                if shift is not None:
                    here = here - shift
                own[el] = y + x * here + (z + pltpu.roll(z, 64, 1))

        copies[0].wait()
        copies[1].wait()

        @pl.when(has_above)
        def _():
            copies[2].wait_send()
            copies[3].wait_recv()

        @pl.when(has_below)
        def _():
            copies[3].wait_send()
            copies[2].wait_recv()

        for p in range(2):
            for k in range(4):
                e = 4 * p + k
                field[e + 1] = pltpu.roll(halo_in[parity, p], (48 - 16 * k) % 128, 1)
                field[5 * 10 + e + 1] = pltpu.roll(halo_in[parity, 2 + p], (128 - 16 * k) % 128, 1)

        @pl.when(has_below)
        def _():
            for k in range(A_ROWS):
                field[(k + 1) * 10] = pltpu.roll(halo_in[parity, 4], 3 - k, 1)

        @pl.when(has_above)
        def _():
            for k in range(A_ROWS):
                field[(k + 1) * 10 + E_ROWS + 1] = pltpu.roll(
                    halo_in[parity, 5], (128 - k) % 128, 1
                )

        @pl.loop(0, ELEMS // 4)
        def _(group):
            vectors = []
            for k in range(4):
                el = group * 4 + k
                at = padded(el)
                sideways = jnp.where(
                    node_x == 3,
                    kappa_pad[pl.ds(at - 10, 1), :] * field[at - 10],
                    kappa_x[pl.ds(el, 1), :] * field[at + 10],
                )
                upright = jnp.where(
                    node_z == 3,
                    kappa_pad[pl.ds(at - 1, 1), :] * field[at - 1],
                    kappa_z[pl.ds(el, 1), :] * field[at + 1],
                )
                vectors.append(jnp.concatenate([sideways, upright], axis=1))
            ch, cl = split(jnp.concatenate(vectors, axis=0))
            coupled = dot3(ch, cl, m_hi[...], m_lo[...])
            for k in range(4):
                el = group * 4 + k
                w = own[el] - coupled[k * NV : (k + 1) * NV]
                wh, wl = split(w)
                basis_hi[el, slot_out * NV : (slot_out + 1) * NV, :] = wh
                basis_lo[el, slot_out * NV : (slot_out + 1) * NV, :] = wl
                if field_out is not None:
                    field_out[padded(el)] = w

    def gram(step):
        first = 0 if step == 0 else 2 * step + 1
        stop = 2 * step + 3
        rows = (stop - first) * NV
        width = stop * NV

        def body(pair, acc):
            def both(ref, begin, end):
                return jnp.concatenate(
                    [ref[pair * 2, begin:end, :], ref[pair * 2 + 1, begin:end, :]], axis=1
                )

            wh = both(basis_hi, first * NV, stop * NV)
            wl = both(basis_lo, first * NV, stop * NV)
            bh = both(basis_hi, 0, stop * NV)
            bl = both(basis_lo, 0, stop * NV)
            return acc + dot3(wh, wl, bh, bl, NT)

        value = lax.fori_loop(0, ELEMS // 2, body, jnp.zeros((rows, width), f32))
        buffer = sums[step]
        spare = LANES[step] - width
        if spare:
            value = jnp.concatenate([value, jnp.zeros((rows, spare), f32)], axis=1)
        buffer[0:rows, :] = value
        if ROWS[step] > rows:
            buffer[rows:, :] = jnp.zeros((ROWS[step] - rows, LANES[step]), f32)

    def all_sum(step, work):
        size = ROWS[step] // n_dep
        mine = pl.ds(pl.multiple_of(dep * size, 8), size)
        copies_a = []
        for k in range(1, n_dep):
            to = lax.rem(dep + k, n_dep)
            copies_a.append(
                pltpu.make_async_remote_copy(
                    src_ref=sums[step].at[pl.ds(pl.multiple_of(to * size, 8), size)],
                    dst_ref=take_a[step].at[k],
                    send_sem=a_send.at[step, k],
                    recv_sem=a_recv.at[step, k],
                    device_id=(lat, to),
                    device_id_type=MESH,
                )
            )
            copies_a[-1].start()
        if work is not None:
            work()
        value = sums[step][mine, :]
        for k in range(1, n_dep):
            copies_a[k - 1].wait_recv()
            value = value + take_a[step][k]
        part[step][...] = value
        copies_b = []
        for k in range(1, n_lat):
            copies_b.append(
                pltpu.make_async_remote_copy(
                    src_ref=part[step],
                    dst_ref=take_b[step].at[lat],
                    send_sem=b_send.at[step, k],
                    recv_sem=b_recv.at[step, k],
                    device_id=(lax.rem(lat + k, n_lat), dep),
                    device_id_type=MESH,
                )
            )
            copies_b[-1].start()
        take_b[step][lat] = value
        for copy in copies_b:
            copy.wait_recv()
        value = take_b[step][0]
        for k in range(1, n_lat):
            value = value + take_b[step][k]
        total[step][mine, :] = value
        copies_c = []
        for k in range(1, n_dep):
            copies_c.append(
                pltpu.make_async_remote_copy(
                    src_ref=total[step].at[mine],
                    dst_ref=total[step].at[mine],
                    send_sem=c_send.at[step, k],
                    recv_sem=c_recv.at[step, k],
                    device_id=(lat, lax.rem(dep + k, n_dep)),
                    device_id_type=MESH,
                )
            )
            copies_c[-1].start()
        for copy in copies_c:
            copy.wait_recv()
        for copy in copies_a + copies_b + copies_c:
            copy.wait_send()
        return total[step][...]

    def mix(step, table):
        first = 0 if step == 0 else 2 * step + 1
        stop = 2 * step + 3
        th, tl = split(table)

        @pl.loop(0, ELEMS // 2)
        def _(pair):
            def both(ref):
                return jnp.concatenate(
                    [ref[pair * 2, 0 : stop * NV, :], ref[pair * 2 + 1, 0 : stop * NV, :]],
                    axis=1,
                )

            fresh = dot3(th, tl, both(basis_hi), both(basis_lo))
            fh, fl = split(fresh)
            for half in range(2):
                el = pair * 2 + half
                cut = slice(half * 128, half * 128 + 128)
                basis_hi[el, first * NV : stop * NV, :] = fh[:, cut]
                basis_lo[el, first * NV : stop * NV, :] = fl[:, cut]
                field_a[padded(el)] = fresh[-NV:, cut]

    def extend(step):
        new = hess[step * 64 : step * 64 + 64, :]
        rows = dot_exact(new, hess[0 : step * 64 + 64, :], NT)
        right = dot_exact(new[:, 0:NV], ninv[4, 0:NV, 0:NV], NT)
        pieces = []
        for i in range(step):
            block = rows[:, i * 64 : i * 64 + 64]
            for k in range(i):
                block = block - dot_exact(pieces[k], nfac[i, k], NT)
            block = dot_exact(block, ninv[i], NT)
            pieces.append(block)
            nfac[step, i] = block
            right = right - dot_exact(block, ysol[i])
        corner = rows[:, step * 64 : step * 64 + 64]
        for block in pieces:
            corner = corner - dot_exact(block, block, NT)
        _, inverse = eliminate(corner)
        ninv[step] = inverse
        ysol[step] = dot_exact(inverse, right)

    hess[...] = jnp.zeros_like(hess)

    operator(field_a, field_b, 0, 1, None, 0)
    operator(field_b, None, 1, 2, None, 1)
    gram(0)
    table = all_sum(0, None)[0:96, 0:96]
    upper, inverse = eliminate(table)
    mix(0, inverse)
    lower = upper.T
    ninv[4] = jnp.concatenate(
        [jnp.concatenate([lower[0:NV, 0:NV], jnp.zeros((NV, NV), f32)], axis=1), jnp.zeros((NV, 64), f32)],
        axis=0,
    )
    column0 = dot_exact(inverse[0:NV, 0:NV], lower[NV : 2 * NV, :])
    column1 = dot_exact(
        inverse[NV : 2 * NV, NV : 2 * NV],
        lower[2 * NV :, :] - dot_exact(lower[NV : 2 * NV, 0:NV], column0),
    )
    hess[0:NV, 0:96] = column0
    hess[NV : 2 * NV, 0:96] = column1
    shift = jnp.sum(
        jnp.sum(jnp.where(iota((NV, 96), 0) == iota((NV, 96), 1), column0, 0.0), axis=1, keepdims=True),
        axis=0,
        keepdims=True,
    ) * (1.0 / NV)

    for step in range(1, 4):
        known = 2 * step + 1
        operator(field_a, field_b, known - 1, known, shift, 0)
        operator(field_b, None, known, known + 1, shift, 1)
        gram(step)
        table = all_sum(step, functools.partial(extend, step - 1))
        prods = table[:, 0 : known * NV]
        corner = table[:, known * NV : known * NV + 64] - dot_exact(prods, prods, NT)
        upper, inverse = eliminate(corner)
        weights = jnp.concatenate([-dot_exact(inverse, prods), inverse], axis=1)
        if step < 3:
            mix(step, weights)
        lower = upper.T
        width = (known + 2) * NV
        coefs = jnp.concatenate([prods, lower], axis=1)
        place = iota((NV, width), 1) - iota((NV, width), 0)
        first = coefs[0:NV] + jnp.where(place == (known - 1) * NV, shift, 0.0)
        hess[2 * step * NV : 2 * step * NV + NV, 0:width] = first
        second = coefs[NV:] + shift * coefs[0:NV]
        second = second - dot_exact(
            prods[0:NV, :], hess[0 : known * NV, 0:width]
        )
        second = dot_exact(inverse[0:NV, 0:NV], second)
        hess[known * NV : known * NV + NV, 0:width] = second
    extend(3)

    answers = [None] * 4
    for i in range(3, -1, -1):
        value = ysol[i]
        for k in range(i + 1, 4):
            value = value - dot_exact(nfac[k, i].T, answers[k])
        answers[i] = dot_exact(ninv[i].T, value)
    solved = jnp.concatenate(answers, axis=0).T
    final = solved[:, 7 * NV : 8 * NV]
    head = solved[:, 0 : 7 * NV] + dot_exact(final, weights[0:NV, 0 : 7 * NV])
    tail = dot_exact(final, weights[0:NV, 7 * NV : 8 * NV])
    th, tl = split(jnp.concatenate([head, tail], axis=1))

    @pl.loop(0, ELEMS // 2)
    def _(pair):
        def both(ref):
            return jnp.concatenate(
                [ref[pair * 2, 0 : 8 * NV, :], ref[pair * 2 + 1, 0 : 8 * NV, :]], axis=1
            )

        value = dot3(th, tl, both(basis_hi), both(basis_lo))
        out_ref[pair * 2] = value[:, 0:128]
        out_ref[pair * 2 + 1] = value[:, 128:256]


def solution(mesh):
    n_lat, n_dep = mesh.shape["lat"], mesh.shape["dep"]

    def per_device(state, kappa, rate, grads, lift, rhs):
        gt = jnp.concatenate([grads.transpose(2, 0, 1).reshape(64, 192), jnp.zeros((64, 64), f32)], axis=1)
        g = jnp.concatenate([grads.reshape(192, 64), jnp.zeros((64, 64), f32)], axis=0)
        zero = jnp.zeros_like(g)
        ga = jnp.concatenate([g, zero], axis=1)
        gb = jnp.concatenate([zero, g], axis=1)
        by_species = lift.reshape(4, 2, 16, 128)
        gap = jnp.zeros((2, 32, 128), f32)
        m_lat = jnp.concatenate([by_species[1], gap, by_species[0]], axis=1).reshape(128, 128)
        hole = jnp.zeros((32, 2, 128), f32)
        m_dep = jnp.concatenate([lift[3][:, None], hole, lift[2][:, None]], axis=1).reshape(128, 128)
        m = jnp.concatenate([m_lat, m_dep], axis=0)
        vmem = pl.BlockSpec(memory_space=pltpu.VMEM)
        V = pltpu.VMEM
        dma = pltpu.SemaphoreType.DMA
        out = pl.pallas_call(
            functools.partial(kernel, n_lat, n_dep),
            out_shape=jax.ShapeDtypeStruct((ELEMS, NV, 128), f32),
            in_specs=[vmem] * 8,
            out_specs=vmem,
            scratch_shapes=[
                V((ELEMS, 9 * NV, 128), bf16),
                V((ELEMS, 9 * NV, 128), bf16),
                V((ELEMS, 128, 128), bf16),
                V((ELEMS, 128, 128), bf16),
                V((60, NV, 128), f32),
                V((60, NV, 128), f32),
                V((ELEMS, NV, 128), f32),
                V((64, 128), f32),
                V((ELEMS, 128), f32),
                V((ELEMS, 128), f32),
                V((ELEMS, 128), f32),
                V((ELEMS, 128), f32),
                V((256, 128), bf16),
                V((256, 128), bf16),
                V((2, 6, NV, 128), f32),
                V((2, 6, NV, 128), f32),
                V((256, 384), f32),
                V((4, 4, 64, 64), f32),
                V((5, 64, 64), f32),
                V((4, 64, NV), f32),
                [V((ROWS[t], LANES[t]), f32) for t in range(4)],
                [V((n_dep, ROWS[t] // n_dep, LANES[t]), f32) for t in range(4)],
                [V((ROWS[t] // n_dep, LANES[t]), f32) for t in range(4)],
                [V((n_lat, ROWS[t] // n_dep, LANES[t]), f32) for t in range(4)],
                [V((ROWS[t], LANES[t]), f32) for t in range(4)],
                dma((2, 4)),
                dma((2, 4)),
                dma((4, n_dep)),
                dma((4, n_dep)),
                dma((4, n_lat)),
                dma((4, n_lat)),
                dma((4, n_dep)),
                dma((4, n_dep)),
            ],
            compiler_params=pltpu.CompilerParams(
                collective_id=0, has_side_effects=True, vmem_limit_bytes=60 * 1024 * 1024
            ),
        )(
            kappa.reshape(ELEMS, 128),
            state.reshape(ELEMS, 128),
            rate.reshape(ELEMS, 1),
            gt,
            ga,
            gb,
            m,
            rhs.reshape(ELEMS, NV, 128),
        )
        return out.reshape(A_ROWS, E_ROWS, NV, 128)

    in_specs = (
        P("lat", "dep", None),
        P("lat", "dep", None),
        P("lat", "dep"),
        P(),
        P(),
        P("lat", "dep", None, None),
    )
    return jax.shard_map(
        per_device, mesh=mesh, in_specs=in_specs, out_specs=P("lat", "dep", None, None), check_vma=False
    )
```

```python
import functools

import jax
import jax.numpy as jnp
from jax import lax
from jax.experimental import pallas as pl
from jax.experimental.pallas import tpu as pltpu
from jax.sharding import PartitionSpec as P

MESH = pl.DeviceIdType.MESH
highest = lax.Precision.HIGHEST
f32 = jnp.float32
bf16 = jnp.bfloat16

A_ROWS, E_ROWS = 4, 8
ELEMS = A_ROWS * E_ROWS
OWN, PAIR, MIX = 16, 32, 8
NV = 32
STEPS = 3
RAW = 3 * NV
KNOWN = (0, 3, 6)
SUM_ROWS = (128, 192, 320)
CUTS = (0, 64, 160, 256)

NN = (((1,), (0,)), ((), ()))
NT = (((1,), (1,)), ((), ()))


def split(x):
    hi = x.astype(bf16)
    return hi, (x - hi.astype(f32)).astype(bf16)


def dot(a, b, dims=NN):
    return lax.dot_general(a, b, dims, preferred_element_type=f32)


def dot_exact(a, b, dims=NN):
    return lax.dot_general(a, b, dims, precision=highest, preferred_element_type=f32)


def dot3(ah, al, bh, bl, dims=NN):
    rows = ah.shape[0]
    both = dot(jnp.concatenate([ah, al], axis=0), bh, dims)
    return both[:rows] + both[rows:] + dot(ah, bl, dims)


def dot4(ah, al, bh, bl, dims=NN):
    rows = ah.shape[0]
    stacked = jnp.concatenate([ah, al], axis=0)
    high = dot(stacked, bh, dims)
    low = dot(stacked, bl, dims)
    return high[:rows] + (high[rows:] + (low[:rows] + low[rows:]))


def iota(shape, dim):
    return lax.broadcasted_iota(jnp.int32, shape, dim)


def eye(n):
    return (iota((n, n), 0) == iota((n, n), 1)).astype(f32)


class Elimination:
    def __init__(self, gram):
        self.n = gram.shape[0]
        wide = jnp.concatenate([gram, eye(self.n)], axis=1)
        self.tiles = [wide[8 * i : 8 * i + 8] for i in range(self.n // 8)]

    def run(self, begin, end):
        width = 2 * self.n
        row = iota((8, width), 0)

        def column(x, k):
            return jnp.broadcast_to(x[:, k : k + 1], (8, width))

        for k in range(begin, end, 2):
            p, q = k // 8, k % 8
            x = self.tiles[p]
            head0, head1 = column(x, k), column(x, k + 1)
            row0, row1 = x[q : q + 1, :], x[q + 1 : q + 2, :]
            a, b, c = head0[q : q + 1], head1[q : q + 1], head1[q + 1 : q + 2]
            a_inv = 1.0 / a
            det_inv = 1.0 / (a * c - b * b)
            t = b * a_inv
            scaled0 = row0 * a_inv
            scaled1 = (row1 - t * row0) * (a * det_inv)
            for i in range(p, self.n // 8):
                x = self.tiles[i]
                c0 = head0 if i == p else column(x, k)
                c1 = head1 if i == p else column(x, k + 1)
                c1 = c1 - c0 * t
                if i == p:
                    c0 = jnp.where(row > q, c0, 0.0)
                    c1 = jnp.where(row > q + 1, c1, 0.0)
                self.tiles[i] = x - c0 * scaled0 - c1 * scaled1

    def finish(self):
        n, width = self.n, 2 * self.n
        wide = jnp.concatenate(self.tiles, axis=0)
        on_diag = iota((n, width), 0) == iota((n, width), 1)
        pivots = jnp.sum(jnp.where(on_diag, wide, 0.0), axis=1, keepdims=True)
        wide = wide * lax.rsqrt(pivots)
        upper = jnp.where(iota((n, n), 0) <= iota((n, n), 1), wide[:, :n], 0.0)
        return upper, wide[:, n:]


def eliminate(gram):
    work = Elimination(gram)
    work.run(0, work.n)
    return work.finish()


def kernel(
    n_lat,
    n_dep,
    kappa_ref,
    state_ref,
    rate_ref,
    grads_ref,
    lift_ref,
    rhs_ref,
    out_ref,
    basis_hi,
    basis_lo,
    stiff_hi,
    stiff_lo,
    field_a,
    field_b,
    own,
    kappa_pad,
    kappa_x,
    kappa_z,
    diag,
    cross,
    m_hi,
    m_lo,
    halo_out,
    halo_in,
    hess,
    start,
    nfac,
    ninv,
    ysol,
    sums,
    take_a,
    part,
    take_b,
    total,
    halo_send,
    halo_recv,
    a_send,
    a_recv,
    b_send,
    b_recv,
    c_send,
    c_recv,
):
    lat = lax.axis_index("lat")
    dep = lax.axis_index("dep")

    barrier = pltpu.get_barrier_semaphore()
    for k in range(1, n_dep):
        pl.semaphore_signal(
            barrier, inc=1, device_id=(lat, lax.rem(dep + k, n_dep)), device_id_type=MESH
        )
    for k in range(1, n_lat):
        pl.semaphore_signal(
            barrier, inc=1, device_id=(lax.rem(lat + k, n_lat), dep), device_id_type=MESH
        )

    lane = iota((1, 128), 1)
    node_x = lane % 64 // 16
    node_z = lane % 4

    def padded(el):
        return (el // E_ROWS + 1) * 10 + el % E_ROWS + 1

    touches = (node_x == 0) | (node_x == 3)
    touches = touches.astype(f32) + ((node_z == 0) | (node_z == 3)).astype(f32)
    kappa_pad[...] = jnp.ones_like(kappa_pad)
    for a in range(A_ROWS):
        here = slice(a * E_ROWS, (a + 1) * E_ROWS)
        kappa = kappa_ref[a]
        picked = iota((E_ROWS, E_ROWS), 0) == iota((E_ROWS, E_ROWS), 1)
        speed = jnp.sum(jnp.where(picked, rate_ref[a : a + 1, :], 0.0), axis=1, keepdims=True)
        diag[here, :] = 0.25 + kappa * touches
        cross[here, :] = speed * pltpu.roll(state_ref[a], 64, 1)
        kappa_x[here, :] = pltpu.roll(kappa, 80, 1)
        kappa_z[here, :] = pltpu.roll(kappa, 125, 1)
        base = (a + 1) * 10 + 1
        kappa_pad[base : base + E_ROWS, :] = kappa
        for side in (0, E_ROWS + 1):
            field_a[(a + 1) * 10 + side] = jnp.zeros((NV, 128), f32)
            field_b[(a + 1) * 10 + side] = jnp.zeros((NV, 128), f32)

    for a in range(A_ROWS):
        for e in range(E_ROWS):
            el = a * E_ROWS + e
            v = rhs_ref[a, e]
            vh, vl = split(v)
            basis_hi[el, 0:NV, :] = vh
            basis_lo[el, 0:NV, :] = vl
            field_a[padded(el)] = v

    def halo_copies(slot):
        right, left = lax.rem(lat + 1, n_lat), lax.rem(lat + n_lat - 1, n_lat)
        copies = []
        for index, (start, size, where) in enumerate(
            (
                (0, 2, (right, dep)),
                (2, 2, (left, dep)),
                (4, 1, (lat, lax.rem(dep + 1, n_dep))),
                (5, 1, (lat, lax.rem(dep + n_dep - 1, n_dep))),
            )
        ):
            copies.append(
                pltpu.make_async_remote_copy(
                    src_ref=halo_out.at[slot, pl.ds(start, size)],
                    dst_ref=halo_in.at[slot, pl.ds(start, size)],
                    send_sem=halo_send.at[slot, index],
                    recv_sem=halo_recv.at[slot, index],
                    device_id=where,
                    device_id_type=MESH,
                )
            )
        return copies

    has_above = dep < n_dep - 1
    has_below = dep > 0

    def send_faces(field, parity):
        for p in range(2):
            right = None
            left = None
            for k in range(4):
                e = 4 * p + k
                index = 4 * 10 + e + 1
                there = pltpu.roll(
                    field[index] * kappa_pad[index : index + 1, :], (80 + 16 * k) % 128, 1
                )
                back = pltpu.roll(field[10 + e + 1], 16 * k, 1)
                mask = node_x == k
                right = there if right is None else jnp.where(mask, there, right)
                left = back if left is None else jnp.where(mask, back, left)
            halo_out[parity, p] = right
            halo_out[parity, 2 + p] = left
        up = None
        down = None
        for k in range(A_ROWS):
            index = (k + 1) * 10 + E_ROWS
            there = pltpu.roll(
                field[index] * kappa_pad[index : index + 1, :], (125 + k) % 128, 1
            )
            back = pltpu.roll(field[(k + 1) * 10 + 1], k, 1)
            mask = node_z == k
            up = there if up is None else jnp.where(mask, there, up)
            down = back if down is None else jnp.where(mask, back, down)
        halo_out[parity, 4] = up
        halo_out[parity, 5] = down
        copies = halo_copies(parity)
        copies[0].start()
        copies[1].start()

        @pl.when(has_above)
        def _():
            copies[2].start()

        @pl.when(has_below)
        def _():
            copies[3].start()

        return copies

    def operator(field, field_out, slot_in, slot_out, shift, parity, copies):
        @pl.loop(0, ELEMS // OWN)
        def _(group):
            for k in range(OWN):
                el = group * OWN + k
                xh = basis_hi[el, slot_in * NV : (slot_in + 1) * NV, :]
                xl = basis_lo[el, slot_in * NV : (slot_in + 1) * NV, :]
                x = field[padded(el)]
                z = x * cross[pl.ds(el, 1), :]
                y = dot3(xh, xl, stiff_hi[el], stiff_lo[el])
                here = diag[pl.ds(el, 1), :]
                if shift is not None:
                    here = here - shift
                own[el] = y + x * here + (z + pltpu.roll(z, 64, 1))

        copies[0].wait()
        copies[1].wait()

        @pl.when(has_above)
        def _():
            copies[2].wait_send()
            copies[3].wait_recv()

        @pl.when(has_below)
        def _():
            copies[3].wait_send()
            copies[2].wait_recv()

        for p in range(2):
            for k in range(4):
                e = 4 * p + k
                field[e + 1] = pltpu.roll(halo_in[parity, p], (48 - 16 * k) % 128, 1)
                field[5 * 10 + e + 1] = pltpu.roll(halo_in[parity, 2 + p], (128 - 16 * k) % 128, 1)

        @pl.when(has_below)
        def _():
            for k in range(A_ROWS):
                field[(k + 1) * 10] = pltpu.roll(halo_in[parity, 4], 3 - k, 1)

        @pl.when(has_above)
        def _():
            for k in range(A_ROWS):
                field[(k + 1) * 10 + E_ROWS + 1] = pltpu.roll(
                    halo_in[parity, 5], (128 - k) % 128, 1
                )

        @pl.loop(0, ELEMS // PAIR)
        def _(bunch):
            for part_of in range(PAIR // 4):
                vectors = []
                for k in range(4):
                    el = bunch * PAIR + part_of * 4 + k
                    at = padded(el)
                    sideways = jnp.where(
                        node_x == 3,
                        kappa_pad[pl.ds(at - 10, 1), :] * field[at - 10],
                        kappa_x[pl.ds(el, 1), :] * field[at + 10],
                    )
                    upright = jnp.where(
                        node_z == 3,
                        kappa_pad[pl.ds(at - 1, 1), :] * field[at - 1],
                        kappa_z[pl.ds(el, 1), :] * field[at + 1],
                    )
                    vectors.append(jnp.concatenate([sideways, upright], axis=1))
                ch, cl = split(jnp.concatenate(vectors, axis=0))
                coupled = dot3(ch, cl, m_hi[...], m_lo[...])
                for k in range(4):
                    el = bunch * PAIR + part_of * 4 + k
                    w = own[el] - coupled[k * NV : (k + 1) * NV]
                    wh, wl = split(w)
                    basis_hi[el, slot_out * NV : (slot_out + 1) * NV, :] = wh
                    basis_lo[el, slot_out * NV : (slot_out + 1) * NV, :] = wl
                    if field_out is not None:
                        field_out[padded(el)] = w

    def gram(step):
        first = KNOWN[step] * NV
        stop = first + RAW

        def body(quad, acc):
            def four(ref, begin, end):
                return jnp.concatenate([ref[quad * 4 + k, begin:end, :] for k in range(4)], axis=1)

            wh, wl = four(basis_hi, first, stop), four(basis_lo, first, stop)
            bh, bl = four(basis_hi, 0, stop), four(basis_lo, 0, stop)
            return acc + dot4(wh, wl, bh, bl, NT)

        value = lax.fori_loop(0, ELEMS // 4, body, jnp.zeros((RAW, stop), f32))
        for i in range(step + 1):
            piece = value[:, i * 128 : min(i * 128 + 128, stop)]
            spare = 128 - piece.shape[1]
            if spare:
                piece = jnp.concatenate([piece, jnp.zeros((RAW, spare), f32)], axis=1)
            sums[step][i * RAW : (i + 1) * RAW, :] = piece
        used = (step + 1) * RAW
        if SUM_ROWS[step] > used:
            sums[step][used:, :] = jnp.zeros((SUM_ROWS[step] - used, 128), f32)

    def all_sum(step, work):
        size = SUM_ROWS[step] // n_dep
        mine = pl.ds(pl.multiple_of(dep * size, 8), size)
        copies_a = []
        for k in range(1, n_dep):
            to = lax.rem(dep + k, n_dep)
            copies_a.append(
                pltpu.make_async_remote_copy(
                    src_ref=sums[step].at[pl.ds(pl.multiple_of(to * size, 8), size)],
                    dst_ref=take_a[step].at[k],
                    send_sem=a_send.at[step, k],
                    recv_sem=a_recv.at[step, k],
                    device_id=(lat, to),
                    device_id_type=MESH,
                )
            )
            copies_a[-1].start()
        work(0)
        value = sums[step][mine, :]
        for k in range(1, n_dep):
            copies_a[k - 1].wait_recv()
            value = value + take_a[step][k]
        part[step][...] = value
        copies_b = []
        for k in range(1, n_lat):
            copies_b.append(
                pltpu.make_async_remote_copy(
                    src_ref=part[step],
                    dst_ref=take_b[step].at[lat],
                    send_sem=b_send.at[step, k],
                    recv_sem=b_recv.at[step, k],
                    device_id=(lax.rem(lat + k, n_lat), dep),
                    device_id_type=MESH,
                )
            )
            copies_b[-1].start()
        take_b[step][lat] = value
        work(1)
        for copy in copies_b:
            copy.wait_recv()
        value = take_b[step][0]
        for k in range(1, n_lat):
            value = value + take_b[step][k]
        total[step][mine, :] = value
        copies_c = []
        for k in range(1, n_dep):
            copies_c.append(
                pltpu.make_async_remote_copy(
                    src_ref=total[step].at[mine],
                    dst_ref=total[step].at[mine],
                    send_sem=c_send.at[step, k],
                    recv_sem=c_recv.at[step, k],
                    device_id=(lat, lax.rem(dep + k, n_dep)),
                    device_id_type=MESH,
                )
            )
            copies_c[-1].start()
        work(2)
        for copy in copies_c:
            copy.wait_recv()
        for copy in copies_a + copies_b + copies_c:
            copy.wait_send()
        return jnp.concatenate(
            [total[step][i * RAW : (i + 1) * RAW, :] for i in range(step + 1)], axis=1
        )

    def mix(step, table):
        first = KNOWN[step] * NV
        stop = first + RAW
        th, tl = split(table)

        @pl.loop(0, ELEMS // MIX)
        def _(bunch):
            for k in range(0, MIX, 2):
                el = bunch * MIX + k

                def both(ref):
                    return jnp.concatenate([ref[el, 0:stop, :], ref[el + 1, 0:stop, :]], axis=1)

                fresh = dot3(th, tl, both(basis_hi), both(basis_lo))
                fh, fl = split(fresh)
                for half in range(2):
                    cut = slice(half * 128, half * 128 + 128)
                    basis_hi[el + half, first:stop, :] = fh[:, cut]
                    basis_lo[el + half, first:stop, :] = fl[:, cut]
                    field_a[padded(el + half)] = fresh[-NV:, cut]

    def extend(step, metric=None):
        begin, end = CUTS[step], CUTS[step + 1]
        size = end - begin
        state = {}

        def products():
            new = hess[begin:end, :]
            if metric is None:
                rows = dot_exact(new, hess[0:end, :], NT)
            else:
                rows = dot_exact(new[:, 0:192], hess[0:end, 0:192], NT)
            right = dot_exact(new[:, 0:NV], start[...], NT)
            corner = rows[:, begin:end]
            if metric is not None:
                corner = corner + metric
            pieces = []
            for i in range(step):
                block = rows[:, CUTS[i] : CUTS[i + 1]]
                for k in range(i):
                    block = block - dot_exact(pieces[k], nfac[(i, k)][...], NT)
                block = dot_exact(block, ninv[i][...], NT)
                pieces.append(block)
                nfac[(step, i)][...] = block
                right = right - dot_exact(block, ysol[i][...])
            for block in pieces:
                corner = corner - dot_exact(block, block, NT)
            state["right"] = right
            state["work"] = Elimination(corner)

        def last():
            _, inverse = state["work"].finish()
            ninv[step][...] = inverse
            ysol[step][...] = dot_exact(inverse, state["right"])

        def run(stage):
            first, second = size // 4 // 2 * 2, size * 3 // 4 // 2 * 2
            if stage == 0:
                products()
                state["work"].run(0, first)
            elif stage == 1:
                state["work"].run(first, second)
            else:
                state["work"].run(second, size)
                last()

        return run

    def idle(stage):
        if stage == 0:
            hess[...] = jnp.zeros_like(hess)

    pl.semaphore_wait(barrier, n_lat + n_dep - 2)
    copies = send_faces(field_a, 0)

    g = jnp.concatenate([grads_ref[0], grads_ref[1], grads_ref[2], jnp.zeros((64, 64), f32)], axis=0)
    gt = g.T
    gh, gl = split(jnp.concatenate([g, g], axis=1))
    same = (iota((128, 128), 0) < 64) == (iota((128, 128), 1) < 64)
    low_lanes = lane < 64
    none = jnp.zeros((32, 128), f32)
    m_lat = []
    for s in range(2):
        at = slice(s * 16, s * 16 + 16)
        m_lat += [lift_ref[1, at, :], none, lift_ref[0, at, :]]
    place = iota((128, 32), 0) - 4 * iota((128, 32), 1)
    m_dep = dot_exact((place == 3).astype(f32), lift_ref[2]) + dot_exact(
        (place == 0).astype(f32), lift_ref[3]
    )
    mh, ml = split(jnp.concatenate(m_lat + [m_dep], axis=0))
    m_hi[...] = mh
    m_lo[...] = ml

    @pl.loop(0, A_ROWS)
    def _(a):
        for two in range(E_ROWS // 4):
            scaled = []
            for k in range(4):
                row = kappa_ref[a, two * 4 + k : two * 4 + k + 1, :]
                turned = pltpu.roll(row, 64, 1)
                first = jnp.where(low_lanes, row, turned)
                second = jnp.where(low_lanes, turned, row)
                scaled.append(gt * jnp.concatenate([first, first], axis=1))
                scaled.append(gt * jnp.concatenate([second, second], axis=1))
            sh, sl = split(jnp.concatenate(scaled, axis=0))
            blocks = dot3(sh, sl, gh, gl)
            for k in range(4):
                block = jnp.where(same, blocks[k * 128 : (k + 1) * 128], 0.0)
                bh, bl = split(block)
                el = a * E_ROWS + two * 4 + k
                stiff_hi[el] = bh
                stiff_lo[el] = bl

    operator(field_a, field_b, 0, 1, None, 0, copies)
    copies = send_faces(field_b, 1)
    operator(field_b, None, 1, 2, None, 1, copies)
    gram(0)
    table = all_sum(0, idle)[:, 0:RAW]
    upper, inverse = eliminate(table)
    mix(0, inverse)
    copies = send_faces(field_a, 0)
    lower = upper.T
    start[...] = lower[0:NV, 0:NV]
    column0 = dot_exact(inverse[0:NV, 0:NV], lower[NV : 2 * NV, :])
    column1 = dot_exact(
        inverse[NV : 2 * NV, NV : 2 * NV],
        lower[2 * NV :, :] - dot_exact(lower[NV : 2 * NV, 0:NV], column0),
    )
    hess[0:NV, 0:RAW] = column0
    hess[NV : 2 * NV, 0:RAW] = column1
    on_diag = iota((NV, RAW), 0) == iota((NV, RAW), 1)
    shift = jnp.sum(
        jnp.sum(jnp.where(on_diag, column0, 0.0), axis=1, keepdims=True), axis=0, keepdims=True
    ) * (1.0 / NV)

    for step in (1, 2):
        known = KNOWN[step]
        base = known * NV
        width = base + RAW
        operator(field_a, field_b, known - 1, known, shift, 0, copies)
        copies = send_faces(field_b, 1)
        operator(field_b, field_a, known, known + 1, shift, 1, copies)
        copies = send_faces(field_a, 0)
        operator(field_a, None, known + 1, known + 2, shift, 0, copies)
        gram(step)
        table = all_sum(step, extend(step - 1))
        prods = table[:, 0:base]
        corner = table[:, base:width] - dot_exact(prods, prods, NT)
        if step == 1:
            upper, inverse = eliminate(corner)
            mix(step, jnp.concatenate([-dot_exact(inverse, prods), inverse], axis=1))
            copies = send_faces(field_a, 0)
            tail = upper.T
        else:
            tail = eye(RAW)
        coefs = jnp.concatenate([prods, tail], axis=1)
        place = iota((NV, width), 1) - iota((NV, width), 0)
        row = CUTS[step]
        hess[row : row + NV, 0:width] = coefs[0:NV] + jnp.where(place == base - NV, shift, 0.0)
        for k in (1, 2):
            at = slice(k * NV, (k + 1) * NV)
            before = slice((k - 1) * NV, k * NV)
            column = coefs[at] + shift * coefs[before]
            reach = base if step == 2 else base + (k - 1) * NV
            column = column - dot_exact(coefs[before, 0:reach], hess[0:reach, 0:width])
            if step == 1:
                column = dot_exact(inverse[before, before], column)
            hess[row + k * NV : row + (k + 1) * NV, 0:width] = column

    spread = hess[CUTS[2] : CUTS[3], 6 * NV : 9 * NV]
    last = extend(2, dot_exact(dot_exact(spread, corner), spread, NT))
    for stage in range(3):
        last(stage)

    answers = [None] * STEPS
    for i in range(STEPS - 1, -1, -1):
        value = ysol[i][...]
        for k in range(i + 1, STEPS):
            value = value - dot_exact(nfac[(k, i)][...].T, answers[k])
        answers[i] = dot_exact(ninv[i][...].T, value)
    solved = jnp.concatenate(answers, axis=0).T
    tail = solved[:, 6 * NV : 8 * NV]
    head = solved[:, 0 : 6 * NV] - dot_exact(tail, prods[0 : 2 * NV, :])
    th, tl = split(jnp.concatenate([head, tail], axis=1))

    @pl.loop(0, A_ROWS)
    def _(a):
        for k in range(0, E_ROWS, 2):
            el = a * E_ROWS + k

            def both(ref):
                return jnp.concatenate([ref[el, 0 : 8 * NV, :], ref[el + 1, 0 : 8 * NV, :]], axis=1)

            value = dot3(th, tl, both(basis_hi), both(basis_lo))
            out_ref[a, k] = value[:, 0:128]
            out_ref[a, k + 1] = value[:, 128:256]


def solution(mesh):
    n_lat, n_dep = mesh.shape["lat"], mesh.shape["dep"]

    def per_device(state, kappa, rate, grads, lift, rhs):
        vmem = pl.BlockSpec(memory_space=pltpu.VMEM)
        V = pltpu.VMEM
        dma = pltpu.SemaphoreType.DMA
        out = pl.pallas_call(
            functools.partial(kernel, n_lat, n_dep),
            out_shape=jax.ShapeDtypeStruct((A_ROWS, E_ROWS, NV, 128), f32),
            in_specs=[vmem] * 6,
            out_specs=vmem,
            scratch_shapes=[
                V((ELEMS, 9 * NV, 128), bf16),
                V((ELEMS, 9 * NV, 128), bf16),
                V((ELEMS, 128, 128), bf16),
                V((ELEMS, 128, 128), bf16),
                V((60, NV, 128), f32),
                V((60, NV, 128), f32),
                V((ELEMS, NV, 128), f32),
                V((64, 128), f32),
                V((ELEMS, 128), f32),
                V((ELEMS, 128), f32),
                V((ELEMS, 128), f32),
                V((ELEMS, 128), f32),
                V((256, 128), bf16),
                V((256, 128), bf16),
                V((2, 6, NV, 128), f32),
                V((2, 6, NV, 128), f32),
                V((256, 384), f32),
                V((NV, NV), f32),
                {
                    (i, k): V((CUTS[i + 1] - CUTS[i], CUTS[k + 1] - CUTS[k]), f32)
                    for i in range(STEPS)
                    for k in range(i)
                },
                [V((CUTS[i + 1] - CUTS[i], CUTS[i + 1] - CUTS[i]), f32) for i in range(STEPS)],
                [V((CUTS[i + 1] - CUTS[i], NV), f32) for i in range(STEPS)],
                [V((rows, 128), f32) for rows in SUM_ROWS],
                [V((n_dep, rows // n_dep, 128), f32) for rows in SUM_ROWS],
                [V((rows // n_dep, 128), f32) for rows in SUM_ROWS],
                [V((n_lat, rows // n_dep, 128), f32) for rows in SUM_ROWS],
                [V((rows, 128), f32) for rows in SUM_ROWS],
                dma((2, 4)),
                dma((2, 4)),
                dma((STEPS, n_dep)),
                dma((STEPS, n_dep)),
                dma((STEPS, n_lat)),
                dma((STEPS, n_lat)),
                dma((STEPS, n_dep)),
                dma((STEPS, n_dep)),
            ],
            compiler_params=pltpu.CompilerParams(
                collective_id=0, has_side_effects=True, vmem_limit_bytes=60 * 1024 * 1024
            ),
        )(
            kappa, state, rate, grads, lift, rhs
        )
        return out

    in_specs = (
        P("lat", "dep", None),
        P("lat", "dep", None),
        P("lat", "dep"),
        P(),
        P(),
        P("lat", "dep", None, None),
    )
    return jax.shard_map(
        per_device, mesh=mesh, in_specs=in_specs, out_specs=P("lat", "dep", None, None), check_vma=False
    )
```

```python
import functools

import jax
import jax.numpy as jnp
from jax import lax
from jax.experimental import pallas as pl
from jax.experimental.pallas import tpu as pltpu
from jax.sharding import PartitionSpec as P

MESH = pl.DeviceIdType.MESH
highest = lax.Precision.HIGHEST
f32 = jnp.float32
bf16 = jnp.bfloat16

A_ROWS, E_ROWS = 4, 8
ELEMS = A_ROWS * E_ROWS
OWN, PAIR, MIX = 32, 32, 8
FACES = 6
NV = 32
STEPS = 3
RAW = 3 * NV
KNOWN = (0, 3, 6)
SUM_ROWS = (128, 192, 320)
CUTS = (0, 64, 160, 256)

NN = (((1,), (0,)), ((), ()))
NT = (((1,), (1,)), ((), ()))


def split(x):
    hi = x.astype(bf16)
    return hi, (x - hi.astype(f32)).astype(bf16)


def dot(a, b, dims=NN):
    return lax.dot_general(a, b, dims, preferred_element_type=f32)


def dot_exact(a, b, dims=NN):
    return lax.dot_general(a, b, dims, precision=highest, preferred_element_type=f32)


def dot3(ah, al, bh, bl, dims=NN):
    rows = ah.shape[0]
    both = dot(jnp.concatenate([ah, al], axis=0), bh, dims)
    return both[:rows] + both[rows:] + dot(ah, bl, dims)


def dot4(ah, al, bh, bl, dims=NN):
    rows = ah.shape[0]
    stacked = jnp.concatenate([ah, al], axis=0)
    high = dot(stacked, bh, dims)
    low = dot(stacked, bl, dims)
    return high[:rows] + (high[rows:] + (low[:rows] + low[rows:]))


def iota(shape, dim):
    return lax.broadcasted_iota(jnp.int32, shape, dim)


def eye(n):
    return (iota((n, n), 0) == iota((n, n), 1)).astype(f32)


class Elimination:
    def __init__(self, gram):
        self.n = gram.shape[0]
        wide = jnp.concatenate([gram, eye(self.n)], axis=1)
        self.tiles = [wide[8 * i : 8 * i + 8] for i in range(self.n // 8)]

    def run(self, begin, end):
        width = 2 * self.n
        row = iota((8, width), 0)

        def column(x, k):
            return jnp.broadcast_to(x[:, k : k + 1], (8, width))

        for k in range(begin, end, 2):
            p, q = k // 8, k % 8
            x = self.tiles[p]
            head0, head1 = column(x, k), column(x, k + 1)
            row0, row1 = x[q : q + 1, :], x[q + 1 : q + 2, :]
            a, b, c = head0[q : q + 1], head1[q : q + 1], head1[q + 1 : q + 2]
            a_inv = 1.0 / a
            det_inv = 1.0 / (a * c - b * b)
            t = b * a_inv
            scaled0 = row0 * a_inv
            scaled1 = (row1 - t * row0) * (a * det_inv)
            for i in range(p, self.n // 8):
                x = self.tiles[i]
                c0 = head0 if i == p else column(x, k)
                c1 = head1 if i == p else column(x, k + 1)
                c1 = c1 - c0 * t
                if i == p:
                    c0 = jnp.where(row > q, c0, 0.0)
                    c1 = jnp.where(row > q + 1, c1, 0.0)
                self.tiles[i] = x - c0 * scaled0 - c1 * scaled1

    def finish(self):
        n, width = self.n, 2 * self.n
        wide = jnp.concatenate(self.tiles, axis=0)
        on_diag = iota((n, width), 0) == iota((n, width), 1)
        pivots = jnp.sum(jnp.where(on_diag, wide, 0.0), axis=1, keepdims=True)
        wide = wide * lax.rsqrt(pivots)
        upper = jnp.where(iota((n, n), 0) <= iota((n, n), 1), wide[:, :n], 0.0)
        return upper, wide[:, n:]


def eliminate(gram):
    work = Elimination(gram)
    work.run(0, work.n)
    return work.finish()


def kernel(
    n_lat,
    n_dep,
    kappa_ref,
    state_ref,
    rate_ref,
    grads_ref,
    lift_ref,
    rhs_ref,
    out_ref,
    basis_hi,
    basis_lo,
    stiff_hi,
    stiff_lo,
    field_a,
    field_b,
    own,
    kappa_pad,
    kappa_x,
    kappa_z,
    diag,
    cross,
    m_hi,
    m_lo,
    halo_out,
    halo_in,
    halo_mix,
    hess,
    start,
    nfac,
    ninv,
    ysol,
    sums,
    take_a,
    part,
    take_b,
    total,
    halo_send,
    halo_recv,
    a_send,
    a_recv,
    b_send,
    b_recv,
    c_send,
    c_recv,
):
    lat = lax.axis_index("lat")
    dep = lax.axis_index("dep")

    barrier = pltpu.get_barrier_semaphore()
    for k in range(1, n_dep):
        pl.semaphore_signal(
            barrier, inc=1, device_id=(lat, lax.rem(dep + k, n_dep)), device_id_type=MESH
        )
    for k in range(1, n_lat):
        pl.semaphore_signal(
            barrier, inc=1, device_id=(lax.rem(lat + k, n_lat), dep), device_id_type=MESH
        )

    lane = iota((1, 128), 1)
    node_x = lane % 64 // 16
    node_z = lane % 4

    def padded(el):
        return (el // E_ROWS + 1) * 10 + el % E_ROWS + 1

    touches = (node_x == 0) | (node_x == 3)
    touches = touches.astype(f32) + ((node_z == 0) | (node_z == 3)).astype(f32)
    kappa_pad[...] = jnp.ones_like(kappa_pad)
    for a in range(A_ROWS):
        here = slice(a * E_ROWS, (a + 1) * E_ROWS)
        kappa = kappa_ref[a]
        picked = iota((E_ROWS, E_ROWS), 0) == iota((E_ROWS, E_ROWS), 1)
        speed = jnp.sum(jnp.where(picked, rate_ref[a : a + 1, :], 0.0), axis=1, keepdims=True)
        diag[here, :] = 0.25 + kappa * touches
        cross[here, :] = speed * pltpu.roll(state_ref[a], 64, 1)
        kappa_x[here, :] = pltpu.roll(kappa, 80, 1)
        kappa_z[here, :] = pltpu.roll(kappa, 125, 1)
        base = (a + 1) * 10 + 1
        kappa_pad[base : base + E_ROWS, :] = kappa
        for side in (0, E_ROWS + 1):
            field_a[(a + 1) * 10 + side] = jnp.zeros((NV, 128), f32)
            field_b[(a + 1) * 10 + side] = jnp.zeros((NV, 128), f32)

    for p in (4, 5):
        for ref in (basis_hi, basis_lo):
            ref[ELEMS + p, 0 : 6 * NV, :] = jnp.zeros((6 * NV, 128), bf16)
    for a in range(A_ROWS):
        for e in range(E_ROWS):
            el = a * E_ROWS + e
            v = rhs_ref[a, e]
            vh, vl = split(v)
            basis_hi[el, 0:NV, :] = vh
            basis_lo[el, 0:NV, :] = vl
            field_a[padded(el)] = v

    def halo_copies(slot):
        right, left = lax.rem(lat + 1, n_lat), lax.rem(lat + n_lat - 1, n_lat)
        copies = []
        for index, (start, size, where) in enumerate(
            (
                (0, 2, (right, dep)),
                (2, 2, (left, dep)),
                (4, 1, (lat, lax.rem(dep + 1, n_dep))),
                (5, 1, (lat, lax.rem(dep + n_dep - 1, n_dep))),
            )
        ):
            copies.append(
                pltpu.make_async_remote_copy(
                    src_ref=halo_out.at[slot, pl.ds(start, size)],
                    dst_ref=halo_in.at[slot, pl.ds(start, size)],
                    send_sem=halo_send.at[slot, index],
                    recv_sem=halo_recv.at[slot, index],
                    device_id=where,
                    device_id_type=MESH,
                )
            )
        return copies

    has_above = dep < n_dep - 1
    has_below = dep > 0

    def send_faces(field, parity):
        for p in range(2):
            right = None
            left = None
            for k in range(4):
                e = 4 * p + k
                index = 4 * 10 + e + 1
                there = pltpu.roll(
                    field[index] * kappa_pad[index : index + 1, :], (80 + 16 * k) % 128, 1
                )
                back = pltpu.roll(field[10 + e + 1], 16 * k, 1)
                mask = node_x == k
                right = there if right is None else jnp.where(mask, there, right)
                left = back if left is None else jnp.where(mask, back, left)
            halo_out[parity, p] = right
            halo_out[parity, 2 + p] = left
        up = None
        down = None
        for k in range(A_ROWS):
            index = (k + 1) * 10 + E_ROWS
            there = pltpu.roll(
                field[index] * kappa_pad[index : index + 1, :], (125 + k) % 128, 1
            )
            back = pltpu.roll(field[(k + 1) * 10 + 1], k, 1)
            mask = node_z == k
            up = there if up is None else jnp.where(mask, there, up)
            down = back if down is None else jnp.where(mask, back, down)
        halo_out[parity, 4] = up
        halo_out[parity, 5] = down
        copies = halo_copies(parity)
        copies[0].start()
        copies[1].start()

        @pl.when(has_above)
        def _():
            copies[2].start()

        @pl.when(has_below)
        def _():
            copies[3].start()

        return copies

    def receive(copies, parity, slot):
        def keep(p):
            if slot < 6:
                fh, fl = split(halo_in[parity, p])
                basis_hi[ELEMS + p, slot * NV : (slot + 1) * NV, :] = fh
                basis_lo[ELEMS + p, slot * NV : (slot + 1) * NV, :] = fl

        copies[0].wait()
        copies[1].wait()
        for p in range(4):
            keep(p)

        @pl.when(has_above)
        def _():
            copies[2].wait_send()
            copies[3].wait_recv()
            keep(5)

        @pl.when(has_below)
        def _():
            copies[3].wait_send()
            copies[2].wait_recv()
            keep(4)

    def unpack(field, faces):
        for p in range(2):
            for k in range(4):
                e = 4 * p + k
                field[e + 1] = pltpu.roll(faces[p], (48 - 16 * k) % 128, 1)
                field[5 * 10 + e + 1] = pltpu.roll(faces[2 + p], (128 - 16 * k) % 128, 1)

        @pl.when(has_below)
        def _():
            for k in range(A_ROWS):
                field[(k + 1) * 10] = pltpu.roll(faces[4], 3 - k, 1)

        @pl.when(has_above)
        def _():
            for k in range(A_ROWS):
                field[(k + 1) * 10 + E_ROWS + 1] = pltpu.roll(faces[5], (128 - k) % 128, 1)

    def operator(field, field_out, slot_in, slot_out, shift, parity=0, copies=None, fill=lambda: None):
        @pl.loop(0, ELEMS // OWN)
        def _(group):
            for k in range(OWN):
                el = group * OWN + k
                xh = basis_hi[el, slot_in * NV : (slot_in + 1) * NV, :]
                xl = basis_lo[el, slot_in * NV : (slot_in + 1) * NV, :]
                x = field[padded(el)]
                z = x * cross[pl.ds(el, 1), :]
                y = dot3(xh, xl, stiff_hi[el], stiff_lo[el])
                here = diag[pl.ds(el, 1), :]
                if shift is not None:
                    here = here - shift
                own[el] = y + x * here + (z + pltpu.roll(z, 64, 1))

        if copies is None:
            unpack(field, halo_mix)
        else:
            fill()
            receive(copies, parity, slot_in)
            unpack(field, halo_in.at[parity])

        @pl.loop(0, ELEMS // PAIR)
        def _(bunch):
            for part_of in range(PAIR // 4):
                vectors = []
                for k in range(4):
                    el = bunch * PAIR + part_of * 4 + k
                    at = padded(el)
                    sideways = jnp.where(
                        node_x == 3,
                        kappa_pad[pl.ds(at - 10, 1), :] * field[at - 10],
                        kappa_x[pl.ds(el, 1), :] * field[at + 10],
                    )
                    upright = jnp.where(
                        node_z == 3,
                        kappa_pad[pl.ds(at - 1, 1), :] * field[at - 1],
                        kappa_z[pl.ds(el, 1), :] * field[at + 1],
                    )
                    vectors.append(jnp.concatenate([sideways, upright], axis=1))
                ch, cl = split(jnp.concatenate(vectors, axis=0))
                coupled = dot3(ch, cl, m_hi[...], m_lo[...])
                for k in range(4):
                    el = bunch * PAIR + part_of * 4 + k
                    w = own[el] - coupled[k * NV : (k + 1) * NV]
                    wh, wl = split(w)
                    basis_hi[el, slot_out * NV : (slot_out + 1) * NV, :] = wh
                    basis_lo[el, slot_out * NV : (slot_out + 1) * NV, :] = wl
                    if field_out is not None:
                        field_out[padded(el)] = w

    def gram(step, begin, end):
        known = KNOWN[step] * NV
        first, stop = known + begin * NV, known + end * NV
        rows = slice(begin * NV, end * NV)

        def body(octet, acc):
            def wide(ref, lower, upper):
                return jnp.concatenate([ref[octet * 8 + k, lower:upper, :] for k in range(8)], axis=1)

            wh, wl = wide(basis_hi, first, stop), wide(basis_lo, first, stop)
            bh, bl = wide(basis_hi, 0, stop), wide(basis_lo, 0, stop)
            return acc + dot4(wh, wl, bh, bl, NT)

        value = lax.fori_loop(0, ELEMS // 8, body, jnp.zeros((stop - first, stop), f32))
        for i in range(step + 1):
            filled = max(0, min(128, stop - i * 128))
            parts = [value[:, i * 128 : i * 128 + filled]] if filled else []
            if filled < 128:
                parts.append(jnp.zeros((stop - first, 128 - filled), f32))
            piece = jnp.concatenate(parts, axis=1) if len(parts) > 1 else parts[0]
            sums[step][i * RAW + begin * NV : i * RAW + end * NV, :] = piece

    def settle(table):
        upper = (iota((RAW, RAW), 0) < 2 * NV) & (iota((RAW, RAW), 1) >= 2 * NV)
        return jnp.where(upper, table.T, table)

    def all_sum(step, work):
        size = SUM_ROWS[step] // n_dep
        mine = pl.ds(pl.multiple_of(dep * size, 8), size)
        copies_a = []
        for k in range(1, n_dep):
            to = lax.rem(dep + k, n_dep)
            copies_a.append(
                pltpu.make_async_remote_copy(
                    src_ref=sums[step].at[pl.ds(pl.multiple_of(to * size, 8), size)],
                    dst_ref=take_a[step].at[k],
                    send_sem=a_send.at[step, k],
                    recv_sem=a_recv.at[step, k],
                    device_id=(lat, to),
                    device_id_type=MESH,
                )
            )
            copies_a[-1].start()
        work(0)
        value = sums[step][mine, :]
        for k in range(1, n_dep):
            copies_a[k - 1].wait_recv()
            value = value + take_a[step][k]
        part[step][...] = value
        copies_b = []
        for k in range(1, n_lat):
            copies_b.append(
                pltpu.make_async_remote_copy(
                    src_ref=part[step],
                    dst_ref=take_b[step].at[lat],
                    send_sem=b_send.at[step, k],
                    recv_sem=b_recv.at[step, k],
                    device_id=(lax.rem(lat + k, n_lat), dep),
                    device_id_type=MESH,
                )
            )
            copies_b[-1].start()
        take_b[step][lat] = value
        work(1)
        for copy in copies_b:
            copy.wait_recv()
        value = take_b[step][0]
        for k in range(1, n_lat):
            value = value + take_b[step][k]
        total[step][mine, :] = value
        copies_c = []
        for k in range(1, n_dep):
            copies_c.append(
                pltpu.make_async_remote_copy(
                    src_ref=total[step].at[mine],
                    dst_ref=total[step].at[mine],
                    send_sem=c_send.at[step, k],
                    recv_sem=c_recv.at[step, k],
                    device_id=(lat, lax.rem(dep + k, n_dep)),
                    device_id_type=MESH,
                )
            )
            copies_c[-1].start()
        work(2)
        for copy in copies_c:
            copy.wait_recv()
        for copy in copies_a + copies_b + copies_c:
            copy.wait_send()
        return jnp.concatenate(
            [total[step][i * RAW : (i + 1) * RAW, :] for i in range(step + 1)], axis=1
        )

    def mix(table, first, stop, reach, to_field=True):
        th, tl = split(table)

        def two(el, ghost):
            def both(ref):
                return jnp.concatenate(
                    [ref[el, 0 : reach * NV, :], ref[el + 1, 0 : reach * NV, :]], axis=1
                )

            fresh = dot3(th, tl, both(basis_hi), both(basis_lo))
            fh, fl = split(fresh)
            for half in range(2):
                cut = slice(half * 128, half * 128 + 128)
                basis_hi[el + half, first * NV : stop * NV, :] = fh[:, cut]
                basis_lo[el + half, first * NV : stop * NV, :] = fl[:, cut]
                if to_field and ghost:
                    halo_mix[el + half - ELEMS] = fresh[:, cut]
                elif to_field:
                    field_a[padded(el + half)] = fresh[:, cut]

        @pl.loop(0, ELEMS // MIX)
        def _(bunch):
            for k in range(0, MIX, 2):
                two(bunch * MIX + k, False)

        for p in range(0, FACES, 2):
            two(ELEMS + p, True)

    def extend(step, metric=None):
        begin, end = CUTS[step], CUTS[step + 1]
        size = end - begin
        state = {}

        def products():
            new = hess[begin:end, :]
            if metric is None:
                rows = dot_exact(new, hess[0:end, :], NT)
            else:
                rows = dot_exact(new[:, 0:192], hess[0:end, 0:192], NT)
            right = dot_exact(new[:, 0:NV], start[...], NT)
            corner = rows[:, begin:end]
            if metric is not None:
                corner = corner + metric
            pieces = []
            for i in range(step):
                block = rows[:, CUTS[i] : CUTS[i + 1]]
                for k in range(i):
                    block = block - dot_exact(pieces[k], nfac[(i, k)][...], NT)
                block = dot_exact(block, ninv[i][...], NT)
                pieces.append(block)
                nfac[(step, i)][...] = block
                right = right - dot_exact(block, ysol[i][...])
            for block in pieces:
                corner = corner - dot_exact(block, block, NT)
            state["right"] = right
            state["work"] = Elimination(corner)

        def last():
            _, inverse = state["work"].finish()
            ninv[step][...] = inverse
            ysol[step][...] = dot_exact(inverse, state["right"])

        def run(stage):
            first, second = size // 4 // 2 * 2, size * 3 // 4 // 2 * 2
            if stage == 0:
                products()
                state["work"].run(0, first)
            elif stage == 1:
                state["work"].run(first, second)
            else:
                state["work"].run(second, size)
                last()

        return run

    def idle(stage):
        if stage == 0:
            hess[...] = jnp.zeros_like(hess)

    for step in range(STEPS):
        used = (step + 1) * RAW
        if SUM_ROWS[step] > used:
            sums[step][used:, :] = jnp.zeros((SUM_ROWS[step] - used, 128), f32)

    pl.semaphore_wait(barrier, n_lat + n_dep - 2)
    copies = send_faces(field_a, 0)

    g = jnp.concatenate([grads_ref[0], grads_ref[1], grads_ref[2], jnp.zeros((64, 64), f32)], axis=0)
    gt = g.T
    gh, gl = split(jnp.concatenate([g, g], axis=1))
    same = (iota((128, 128), 0) < 64) == (iota((128, 128), 1) < 64)
    low_lanes = lane < 64
    none = jnp.zeros((32, 128), f32)
    m_lat = []
    for s in range(2):
        at = slice(s * 16, s * 16 + 16)
        m_lat += [lift_ref[1, at, :], none, lift_ref[0, at, :]]
    place = iota((128, 32), 0) - 4 * iota((128, 32), 1)
    m_dep = dot_exact((place == 3).astype(f32), lift_ref[2]) + dot_exact(
        (place == 0).astype(f32), lift_ref[3]
    )
    mh, ml = split(jnp.concatenate(m_lat + [m_dep], axis=0))
    m_hi[...] = mh
    m_lo[...] = ml

    @pl.loop(0, A_ROWS)
    def _(a):
        for two in range(E_ROWS // 4):
            scaled = []
            for k in range(4):
                row = kappa_ref[a, two * 4 + k : two * 4 + k + 1, :]
                turned = pltpu.roll(row, 64, 1)
                first = jnp.where(low_lanes, row, turned)
                second = jnp.where(low_lanes, turned, row)
                scaled.append(gt * jnp.concatenate([first, first], axis=1))
                scaled.append(gt * jnp.concatenate([second, second], axis=1))
            sh, sl = split(jnp.concatenate(scaled, axis=0))
            blocks = dot3(sh, sl, gh, gl)
            for k in range(4):
                block = jnp.where(same, blocks[k * 128 : (k + 1) * 128], 0.0)
                bh, bl = split(block)
                el = a * E_ROWS + two * 4 + k
                stiff_hi[el] = bh
                stiff_lo[el] = bl

    operator(field_a, field_b, 0, 1, None, 0, copies)
    copies = send_faces(field_b, 1)
    operator(field_b, field_a, 1, 2, None, 1, copies, lambda: gram(0, 0, 2))
    copies = send_faces(field_a, 0)
    gram(0, 2, 3)
    table = settle(all_sum(0, idle)[:, 0:RAW])
    upper, inverse = eliminate(table)
    receive(copies, 0, 2)
    mix(inverse[2 * NV :], 2, 3, 3)
    shift = jnp.sum(
        jnp.sum(inverse[0:NV, 0:NV] * upper[0:NV, NV : 2 * NV], axis=1, keepdims=True),
        axis=0,
        keepdims=True,
    ) * (1.0 / NV)

    def record_first():
        lower = upper.T
        start[...] = lower[0:NV, 0:NV]
        column0 = dot_exact(inverse[0:NV, 0:NV], lower[NV : 2 * NV, :])
        column1 = dot_exact(
            inverse[NV : 2 * NV, NV : 2 * NV],
            lower[2 * NV :, :] - dot_exact(lower[NV : 2 * NV, 0:NV], column0),
        )
        hess[0:NV, 0:RAW] = column0
        hess[NV : 2 * NV, 0:RAW] = column1
        mix(inverse[0 : 2 * NV, 0 : 2 * NV], 0, 2, 2, False)

    def record(step, prods, tail, inverse):
        known = KNOWN[step]
        base = known * NV
        width = base + RAW
        coefs = jnp.concatenate([prods, tail], axis=1)
        place = iota((NV, width), 1) - iota((NV, width), 0)
        row = CUTS[step]
        hess[row : row + NV, 0:width] = coefs[0:NV] + jnp.where(place == base - NV, shift, 0.0)
        for k in (1, 2):
            at = slice(k * NV, (k + 1) * NV)
            before = slice((k - 1) * NV, k * NV)
            column = coefs[at] + shift * coefs[before]
            reach = base if inverse is None else base + (k - 1) * NV
            column = column - dot_exact(coefs[before, 0:reach], hess[0:reach, 0:width])
            if inverse is not None:
                column = dot_exact(inverse[before, before], column)
            hess[row + k * NV : row + (k + 1) * NV, 0:width] = column

    def images(step, parity, field_last, fill):
        known = KNOWN[step]
        operator(field_a, field_b, known - 1, known, shift)
        copies = send_faces(field_b, parity)
        operator(field_b, field_a, known, known + 1, shift, parity, copies, fill)
        copies = send_faces(field_a, 1 - parity)
        operator(
            field_a, field_last, known + 1, known + 2, shift, 1 - parity, copies, lambda: gram(step, 0, 2)
        )

    images(1, 1, field_b, record_first)
    copies = send_faces(field_b, 1)
    gram(1, 2, 3)
    table = all_sum(1, extend(0))
    prods = table[:, 0 : 3 * NV]
    corner = settle(table[:, 3 * NV : 6 * NV]) - dot_exact(prods, prods, NT)
    upper, inverse = eliminate(corner)
    receive(copies, 1, 5)
    weights = jnp.concatenate([-dot_exact(inverse, prods), inverse], axis=1)
    mix(weights[2 * NV :], 5, 6, 6)

    def record_second():
        record(1, prods, upper.T, inverse)
        mix(weights[0 : 2 * NV, 0 : 5 * NV], 3, 5, 5, False)

    images(2, 0, None, record_second)
    gram(2, 2, 3)
    table = all_sum(2, extend(1))
    prods = table[:, 0 : 6 * NV]
    corner = settle(table[:, 6 * NV : 9 * NV]) - dot_exact(prods, prods, NT)
    record(2, prods, eye(RAW), None)

    spread = hess[CUTS[2] : CUTS[3], 6 * NV : 9 * NV]
    last = extend(2, dot_exact(dot_exact(spread, corner), spread, NT))
    for stage in range(3):
        last(stage)

    answers = [None] * STEPS
    for i in range(STEPS - 1, -1, -1):
        value = ysol[i][...]
        for k in range(i + 1, STEPS):
            value = value - dot_exact(nfac[(k, i)][...].T, answers[k])
        answers[i] = dot_exact(ninv[i][...].T, value)
    solved = jnp.concatenate(answers, axis=0).T
    tail = solved[:, 6 * NV : 8 * NV]
    head = solved[:, 0 : 6 * NV] - dot_exact(tail, prods[0 : 2 * NV, :])
    th, tl = split(jnp.concatenate([head, tail], axis=1))

    @pl.loop(0, A_ROWS)
    def _(a):
        for k in range(0, E_ROWS, 2):
            el = a * E_ROWS + k

            def both(ref):
                return jnp.concatenate([ref[el, 0 : 8 * NV, :], ref[el + 1, 0 : 8 * NV, :]], axis=1)

            value = dot3(th, tl, both(basis_hi), both(basis_lo))
            out_ref[a, k] = value[:, 0:128]
            out_ref[a, k + 1] = value[:, 128:256]


def solution(mesh):
    n_lat, n_dep = mesh.shape["lat"], mesh.shape["dep"]

    def per_device(state, kappa, rate, grads, lift, rhs):
        vmem = pl.BlockSpec(memory_space=pltpu.VMEM)
        V = pltpu.VMEM
        dma = pltpu.SemaphoreType.DMA
        out = pl.pallas_call(
            functools.partial(kernel, n_lat, n_dep),
            out_shape=jax.ShapeDtypeStruct((A_ROWS, E_ROWS, NV, 128), f32),
            in_specs=[vmem] * 6,
            out_specs=vmem,
            scratch_shapes=[
                V((ELEMS + FACES, 9 * NV, 128), bf16),
                V((ELEMS + FACES, 9 * NV, 128), bf16),
                V((ELEMS, 128, 128), bf16),
                V((ELEMS, 128, 128), bf16),
                V((60, NV, 128), f32),
                V((60, NV, 128), f32),
                V((ELEMS, NV, 128), f32),
                V((64, 128), f32),
                V((ELEMS, 128), f32),
                V((ELEMS, 128), f32),
                V((ELEMS, 128), f32),
                V((ELEMS, 128), f32),
                V((256, 128), bf16),
                V((256, 128), bf16),
                V((2, FACES, NV, 128), f32),
                V((2, FACES, NV, 128), f32),
                V((FACES, NV, 128), f32),
                V((256, 384), f32),
                V((NV, NV), f32),
                {
                    (i, k): V((CUTS[i + 1] - CUTS[i], CUTS[k + 1] - CUTS[k]), f32)
                    for i in range(STEPS)
                    for k in range(i)
                },
                [V((CUTS[i + 1] - CUTS[i], CUTS[i + 1] - CUTS[i]), f32) for i in range(STEPS)],
                [V((CUTS[i + 1] - CUTS[i], NV), f32) for i in range(STEPS)],
                [V((rows, 128), f32) for rows in SUM_ROWS],
                [V((n_dep, rows // n_dep, 128), f32) for rows in SUM_ROWS],
                [V((rows // n_dep, 128), f32) for rows in SUM_ROWS],
                [V((n_lat, rows // n_dep, 128), f32) for rows in SUM_ROWS],
                [V((rows, 128), f32) for rows in SUM_ROWS],
                dma((2, 4)),
                dma((2, 4)),
                dma((STEPS, n_dep)),
                dma((STEPS, n_dep)),
                dma((STEPS, n_lat)),
                dma((STEPS, n_lat)),
                dma((STEPS, n_dep)),
                dma((STEPS, n_dep)),
            ],
            compiler_params=pltpu.CompilerParams(
                collective_id=0, has_side_effects=True, vmem_limit_bytes=60 * 1024 * 1024
            ),
        )(
            kappa, state, rate, grads, lift, rhs
        )
        return out

    in_specs = (
        P("lat", "dep", None),
        P("lat", "dep", None),
        P("lat", "dep"),
        P(),
        P(),
        P("lat", "dep", None, None),
    )
    return jax.shard_map(
        per_device, mesh=mesh, in_specs=in_specs, out_specs=P("lat", "dep", None, None), check_vma=False
    )
```

```python
import functools

import jax
import jax.numpy as jnp
from jax import lax
from jax.experimental import pallas as pl
from jax.experimental.pallas import tpu as pltpu
from jax.sharding import PartitionSpec as P

MESH = pl.DeviceIdType.MESH
highest = lax.Precision.HIGHEST
f32 = jnp.float32
bf16 = jnp.bfloat16

A_ROWS, E_ROWS = 4, 8
ELEMS = A_ROWS * E_ROWS
OWN, PAIR, MIX = 32, 32, 8
FACES = 6
NV = 32
STEPS = 3
RAW = 3 * NV
KNOWN = (0, 3, 6)
SUM_ROWS = (128, 192, 320)
CUTS = (0, 64, 160, 256)

NN = (((1,), (0,)), ((), ()))
NT = (((1,), (1,)), ((), ()))


def split(x):
    hi = x.astype(bf16)
    return hi, (x - hi.astype(f32)).astype(bf16)


def dot(a, b, dims=NN):
    return lax.dot_general(a, b, dims, preferred_element_type=f32)


def dot_exact(a, b, dims=NN):
    return lax.dot_general(a, b, dims, precision=highest, preferred_element_type=f32)


def dot3(ah, al, bh, bl, dims=NN):
    rows = ah.shape[0]
    both = dot(jnp.concatenate([ah, al], axis=0), bh, dims)
    return both[:rows] + both[rows:] + dot(ah, bl, dims)


def dot_wide(ah, al, both):
    first = dot(ah, both)
    return first[:, 0:128] + (first[:, 128:256] + dot(al, both[:, 0:128]))


def dot4(ah, al, bh, bl, dims=NN):
    rows = ah.shape[0]
    stacked = jnp.concatenate([ah, al], axis=0)
    high = dot(stacked, bh, dims)
    low = dot(stacked, bl, dims)
    return high[:rows] + (high[rows:] + (low[:rows] + low[rows:]))


def iota(shape, dim):
    return lax.broadcasted_iota(jnp.int32, shape, dim)


def eye(n):
    return (iota((n, n), 0) == iota((n, n), 1)).astype(f32)


class Elimination:
    def __init__(self, gram):
        self.n = gram.shape[0]
        wide = jnp.concatenate([gram, eye(self.n)], axis=1)
        self.tiles = [wide[8 * i : 8 * i + 8] for i in range(self.n // 8)]

    def run(self, begin, end):
        width = 2 * self.n
        row = iota((8, width), 0)

        def column(x, k):
            return jnp.broadcast_to(x[:, k : k + 1], (8, width))

        for k in range(begin, end, 4):
            p, q = k // 8, k % 8
            x = self.tiles[p]
            head = [column(x, k + j) for j in range(4)]
            row0, row1, row2, row3 = (x[q + j : q + j + 1, :] for j in range(4))
            a, b, c = head[0][q : q + 1], head[1][q : q + 1], head[1][q + 1 : q + 2]
            a_inv = 1.0 / a
            t = b * a_inv
            d_inv = a * (1.0 / (a * c - b * b))
            scaled0 = row0 * a_inv
            scaled1 = (row1 - t * row0) * d_inv
            f02, f03 = head[2][q : q + 1] * a_inv, head[3][q : q + 1] * a_inv
            f12 = (head[2][q + 1 : q + 2] - t * head[2][q : q + 1]) * d_inv
            f13 = (head[3][q + 1 : q + 2] - t * head[3][q : q + 1]) * d_inv

            def reduced(columns):
                c0, c1, c2, c3 = columns
                c1 = c1 - c0 * t
                return c0, c1, c2 - c0 * f02 - c1 * f12, c3 - c0 * f03 - c1 * f13

            h0, h1, h2, h3 = reduced(head)
            row2 = row2 - h0[q + 2 : q + 3] * scaled0 - h1[q + 2 : q + 3] * scaled1
            row3 = row3 - h0[q + 3 : q + 4] * scaled0 - h1[q + 3 : q + 4] * scaled1
            a, b, c = h2[q + 2 : q + 3], h3[q + 2 : q + 3], h3[q + 3 : q + 4]
            a_inv = 1.0 / a
            t2 = b * a_inv
            d_inv = a * (1.0 / (a * c - b * b))
            scaled2 = row2 * a_inv
            scaled3 = (row3 - t2 * row2) * d_inv
            for i in range(p, self.n // 8):
                x = self.tiles[i]
                if i == p:
                    c0, c1, c2, c3 = h0, h1, h2, h3 - h2 * t2
                    c0 = jnp.where(row > q, c0, 0.0)
                    c1 = jnp.where(row > q + 1, c1, 0.0)
                    c2 = jnp.where(row > q + 2, c2, 0.0)
                    c3 = jnp.where(row > q + 3, c3, 0.0)
                else:
                    c0, c1, c2, c3 = reduced([column(x, k + j) for j in range(4)])
                    c3 = c3 - c2 * t2
                self.tiles[i] = x - c0 * scaled0 - c1 * scaled1 - c2 * scaled2 - c3 * scaled3

    def finish(self):
        n, width = self.n, 2 * self.n
        wide = jnp.concatenate(self.tiles, axis=0)
        on_diag = iota((n, width), 0) == iota((n, width), 1)
        pivots = jnp.sum(jnp.where(on_diag, wide, 0.0), axis=1, keepdims=True)
        wide = wide * lax.rsqrt(pivots)
        upper = jnp.where(iota((n, n), 0) <= iota((n, n), 1), wide[:, :n], 0.0)
        return upper, wide[:, n:]


def eliminate(gram):
    work = Elimination(gram)
    work.run(0, work.n)
    return work.finish()


def kernel(
    n_lat,
    n_dep,
    kappa_ref,
    state_ref,
    rate_ref,
    grads_ref,
    lift_ref,
    rhs_ref,
    out_ref,
    basis_hi,
    basis_lo,
    stiff,
    field_a,
    field_b,
    own,
    kappa_pad,
    kappa_x,
    kappa_z,
    diag,
    cross,
    lift_both,
    halo_out,
    halo_in,
    halo_mix,
    hess,
    start,
    nfac,
    ninv,
    ysol,
    sums,
    take_a,
    part,
    take_b,
    total,
    halo_send,
    halo_recv,
    a_send,
    a_recv,
    b_send,
    b_recv,
    c_send,
    c_recv,
):
    lat = lax.axis_index("lat")
    dep = lax.axis_index("dep")

    barrier = pltpu.get_barrier_semaphore()
    for k in range(1, n_dep):
        pl.semaphore_signal(
            barrier, inc=1, device_id=(lat, lax.rem(dep + k, n_dep)), device_id_type=MESH
        )
    for k in range(1, n_lat):
        pl.semaphore_signal(
            barrier, inc=1, device_id=(lax.rem(lat + k, n_lat), dep), device_id_type=MESH
        )

    lane = iota((1, 128), 1)
    node_x = lane % 64 // 16
    node_z = lane % 4

    def padded(el):
        return (el // E_ROWS + 1) * 10 + el % E_ROWS + 1

    touches = (node_x == 0) | (node_x == 3)
    touches = touches.astype(f32) + ((node_z == 0) | (node_z == 3)).astype(f32)
    kappa_pad[...] = jnp.ones_like(kappa_pad)
    for a in range(A_ROWS):
        here = slice(a * E_ROWS, (a + 1) * E_ROWS)
        kappa = kappa_ref[a]
        picked = iota((E_ROWS, E_ROWS), 0) == iota((E_ROWS, E_ROWS), 1)
        speed = jnp.sum(jnp.where(picked, rate_ref[a : a + 1, :], 0.0), axis=1, keepdims=True)
        diag[here, :] = 0.25 + kappa * touches
        cross[here, :] = speed * pltpu.roll(state_ref[a], 64, 1)
        kappa_x[here, :] = pltpu.roll(kappa, 80, 1)
        kappa_z[here, :] = pltpu.roll(kappa, 125, 1)
        base = (a + 1) * 10 + 1
        kappa_pad[base : base + E_ROWS, :] = kappa
        for side in (0, E_ROWS + 1):
            field_a[(a + 1) * 10 + side] = jnp.zeros((NV, 128), f32)
            field_b[(a + 1) * 10 + side] = jnp.zeros((NV, 128), f32)

    for p in (4, 5):
        for ref in (basis_hi, basis_lo):
            ref[ELEMS + p, 0 : 6 * NV, :] = jnp.zeros((6 * NV, 128), bf16)
    for a in range(A_ROWS):
        for e in range(E_ROWS):
            el = a * E_ROWS + e
            v = rhs_ref[a, e]
            vh, vl = split(v)
            basis_hi[el, 0:NV, :] = vh
            basis_lo[el, 0:NV, :] = vl
            field_a[padded(el)] = v

    def halo_copies(slot):
        right, left = lax.rem(lat + 1, n_lat), lax.rem(lat + n_lat - 1, n_lat)
        copies = []
        for index, (start, size, where) in enumerate(
            (
                (0, 2, (right, dep)),
                (2, 2, (left, dep)),
                (4, 1, (lat, lax.rem(dep + 1, n_dep))),
                (5, 1, (lat, lax.rem(dep + n_dep - 1, n_dep))),
            )
        ):
            copies.append(
                pltpu.make_async_remote_copy(
                    src_ref=halo_out.at[slot, pl.ds(start, size)],
                    dst_ref=halo_in.at[slot, pl.ds(start, size)],
                    send_sem=halo_send.at[slot, index],
                    recv_sem=halo_recv.at[slot, index],
                    device_id=where,
                    device_id_type=MESH,
                )
            )
        return copies

    has_above = dep < n_dep - 1
    has_below = dep > 0

    def send_faces(field, parity):
        for p in range(2):
            right = None
            left = None
            for k in range(4):
                e = 4 * p + k
                index = 4 * 10 + e + 1
                there = pltpu.roll(
                    field[index] * kappa_pad[index : index + 1, :], (80 + 16 * k) % 128, 1
                )
                back = pltpu.roll(field[10 + e + 1], 16 * k, 1)
                mask = node_x == k
                right = there if right is None else jnp.where(mask, there, right)
                left = back if left is None else jnp.where(mask, back, left)
            halo_out[parity, p] = right
            halo_out[parity, 2 + p] = left
        up = None
        down = None
        for k in range(A_ROWS):
            index = (k + 1) * 10 + E_ROWS
            there = pltpu.roll(
                field[index] * kappa_pad[index : index + 1, :], (125 + k) % 128, 1
            )
            back = pltpu.roll(field[(k + 1) * 10 + 1], k, 1)
            mask = node_z == k
            up = there if up is None else jnp.where(mask, there, up)
            down = back if down is None else jnp.where(mask, back, down)
        halo_out[parity, 4] = up
        halo_out[parity, 5] = down
        copies = halo_copies(parity)
        copies[0].start()
        copies[1].start()

        @pl.when(has_above)
        def _():
            copies[2].start()

        @pl.when(has_below)
        def _():
            copies[3].start()

        return copies

    def receive(copies, parity, slot):
        def keep(p):
            if slot < 6:
                fh, fl = split(halo_in[parity, p])
                basis_hi[ELEMS + p, slot * NV : (slot + 1) * NV, :] = fh
                basis_lo[ELEMS + p, slot * NV : (slot + 1) * NV, :] = fl

        copies[0].wait()
        copies[1].wait()
        for p in range(4):
            keep(p)

        @pl.when(has_above)
        def _():
            copies[2].wait_send()
            copies[3].wait_recv()
            keep(5)

        @pl.when(has_below)
        def _():
            copies[3].wait_send()
            copies[2].wait_recv()
            keep(4)

    def unpack(field, faces):
        for p in range(2):
            for k in range(4):
                e = 4 * p + k
                field[e + 1] = pltpu.roll(faces[p], (48 - 16 * k) % 128, 1)
                field[5 * 10 + e + 1] = pltpu.roll(faces[2 + p], (128 - 16 * k) % 128, 1)

        @pl.when(has_below)
        def _():
            for k in range(A_ROWS):
                field[(k + 1) * 10] = pltpu.roll(faces[4], 3 - k, 1)

        @pl.when(has_above)
        def _():
            for k in range(A_ROWS):
                field[(k + 1) * 10 + E_ROWS + 1] = pltpu.roll(faces[5], (128 - k) % 128, 1)

    def operator(field, field_out, slot_in, slot_out, shift, parity=0, copies=None, fill=lambda: None):
        @pl.loop(0, ELEMS // OWN)
        def _(group):
            for k in range(OWN):
                el = group * OWN + k
                xh = basis_hi[el, slot_in * NV : (slot_in + 1) * NV, :]
                xl = basis_lo[el, slot_in * NV : (slot_in + 1) * NV, :]
                x = field[padded(el)]
                z = x * cross[pl.ds(el, 1), :]
                y = dot_wide(xh, xl, stiff[el])
                here = diag[pl.ds(el, 1), :]
                if shift is not None:
                    here = here - shift
                own[el] = y + x * here + (z + pltpu.roll(z, 64, 1))

        if copies is None:
            unpack(field, halo_mix)
        else:
            fill()
            receive(copies, parity, slot_in)
            unpack(field, halo_in.at[parity])

        @pl.loop(0, ELEMS // PAIR)
        def _(bunch):
            for part_of in range(PAIR // 4):
                vectors = []
                for k in range(4):
                    el = bunch * PAIR + part_of * 4 + k
                    at = padded(el)
                    sideways = jnp.where(
                        node_x == 3,
                        kappa_pad[pl.ds(at - 10, 1), :] * field[at - 10],
                        kappa_x[pl.ds(el, 1), :] * field[at + 10],
                    )
                    upright = jnp.where(
                        node_z == 3,
                        kappa_pad[pl.ds(at - 1, 1), :] * field[at - 1],
                        kappa_z[pl.ds(el, 1), :] * field[at + 1],
                    )
                    vectors.append(jnp.concatenate([sideways, upright], axis=1))
                ch, cl = split(jnp.concatenate(vectors, axis=0))
                coupled = dot_wide(ch, cl, lift_both[...])
                for k in range(4):
                    el = bunch * PAIR + part_of * 4 + k
                    w = own[el] - coupled[k * NV : (k + 1) * NV]
                    wh, wl = split(w)
                    basis_hi[el, slot_out * NV : (slot_out + 1) * NV, :] = wh
                    basis_lo[el, slot_out * NV : (slot_out + 1) * NV, :] = wl
                    if field_out is not None:
                        field_out[padded(el)] = w

    def gram(step, begin, end):
        known = KNOWN[step] * NV
        first, stop = known + begin * NV, known + end * NV
        rows = slice(begin * NV, end * NV)

        def body(octet, acc):
            def wide(ref, lower, upper):
                return jnp.concatenate([ref[octet * 8 + k, lower:upper, :] for k in range(8)], axis=1)

            wh, wl = wide(basis_hi, first, stop), wide(basis_lo, first, stop)
            bh, bl = wide(basis_hi, 0, stop), wide(basis_lo, 0, stop)
            return acc + dot4(wh, wl, bh, bl, NT)

        value = lax.fori_loop(0, ELEMS // 8, body, jnp.zeros((stop - first, stop), f32))
        for i in range(step + 1):
            filled = max(0, min(128, stop - i * 128))
            parts = [value[:, i * 128 : i * 128 + filled]] if filled else []
            if filled < 128:
                parts.append(jnp.zeros((stop - first, 128 - filled), f32))
            piece = jnp.concatenate(parts, axis=1) if len(parts) > 1 else parts[0]
            sums[step][i * RAW + begin * NV : i * RAW + end * NV, :] = piece

    def settle(table):
        upper = (iota((RAW, RAW), 0) < 2 * NV) & (iota((RAW, RAW), 1) >= 2 * NV)
        return jnp.where(upper, table.T, table)

    def all_sum(step, work):
        size = SUM_ROWS[step] // n_dep
        mine = pl.ds(pl.multiple_of(dep * size, 8), size)
        copies_a = []
        for k in range(1, n_dep):
            to = lax.rem(dep + k, n_dep)
            copies_a.append(
                pltpu.make_async_remote_copy(
                    src_ref=sums[step].at[pl.ds(pl.multiple_of(to * size, 8), size)],
                    dst_ref=take_a[step].at[k],
                    send_sem=a_send.at[step, k],
                    recv_sem=a_recv.at[step, k],
                    device_id=(lat, to),
                    device_id_type=MESH,
                )
            )
            copies_a[-1].start()
        work(0)
        value = sums[step][mine, :]
        for k in range(1, n_dep):
            copies_a[k - 1].wait_recv()
            value = value + take_a[step][k]
        part[step][...] = value
        copies_b = []
        for k in range(1, n_lat):
            copies_b.append(
                pltpu.make_async_remote_copy(
                    src_ref=part[step],
                    dst_ref=take_b[step].at[lat],
                    send_sem=b_send.at[step, k],
                    recv_sem=b_recv.at[step, k],
                    device_id=(lax.rem(lat + k, n_lat), dep),
                    device_id_type=MESH,
                )
            )
            copies_b[-1].start()
        take_b[step][lat] = value
        work(1)
        for copy in copies_b:
            copy.wait_recv()
        value = take_b[step][0]
        for k in range(1, n_lat):
            value = value + take_b[step][k]
        total[step][mine, :] = value
        copies_c = []
        for k in range(1, n_dep):
            copies_c.append(
                pltpu.make_async_remote_copy(
                    src_ref=total[step].at[mine],
                    dst_ref=total[step].at[mine],
                    send_sem=c_send.at[step, k],
                    recv_sem=c_recv.at[step, k],
                    device_id=(lat, lax.rem(dep + k, n_dep)),
                    device_id_type=MESH,
                )
            )
            copies_c[-1].start()
        work(2)
        for copy in copies_c:
            copy.wait_recv()
        for copy in copies_a + copies_b + copies_c:
            copy.wait_send()
        return jnp.concatenate(
            [total[step][i * RAW : (i + 1) * RAW, :] for i in range(step + 1)], axis=1
        )

    def mix(table, first, stop, reach, to_field=True):
        th, tl = split(table)

        def two(el, ghost):
            def both(ref):
                return jnp.concatenate(
                    [ref[el, 0 : reach * NV, :], ref[el + 1, 0 : reach * NV, :]], axis=1
                )

            fresh = dot3(th, tl, both(basis_hi), both(basis_lo))
            fh, fl = split(fresh)
            for half in range(2):
                cut = slice(half * 128, half * 128 + 128)
                basis_hi[el + half, first * NV : stop * NV, :] = fh[:, cut]
                basis_lo[el + half, first * NV : stop * NV, :] = fl[:, cut]
                if to_field and ghost:
                    halo_mix[el + half - ELEMS] = fresh[:, cut]
                elif to_field:
                    field_a[padded(el + half)] = fresh[:, cut]

        @pl.loop(0, ELEMS // MIX)
        def _(bunch):
            for k in range(0, MIX, 2):
                two(bunch * MIX + k, False)

        for p in range(0, FACES, 2):
            two(ELEMS + p, True)

    def extend(step, metric=None):
        begin, end = CUTS[step], CUTS[step + 1]
        size = end - begin
        state = {}

        def products():
            new = hess[begin:end, :]
            if metric is None:
                rows = dot_exact(new, hess[0:end, :], NT)
            else:
                rows = dot_exact(new[:, 0:192], hess[0:end, 0:192], NT)
            right = dot_exact(new[:, 0:NV], start[...], NT)
            corner = rows[:, begin:end]
            if metric is not None:
                corner = corner + metric
            pieces = []
            for i in range(step):
                block = rows[:, CUTS[i] : CUTS[i + 1]]
                for k in range(i):
                    block = block - dot_exact(pieces[k], nfac[(i, k)][...], NT)
                block = dot_exact(block, ninv[i][...], NT)
                pieces.append(block)
                nfac[(step, i)][...] = block
                right = right - dot_exact(block, ysol[i][...])
            for block in pieces:
                corner = corner - dot_exact(block, block, NT)
            state["right"] = right
            state["work"] = Elimination(corner)

        def last():
            _, inverse = state["work"].finish()
            ninv[step][...] = inverse
            ysol[step][...] = dot_exact(inverse, state["right"])

        def run(stage):
            first, second = size // 4 // 4 * 4, size * 3 // 4 // 4 * 4
            if stage == 0:
                products()
                state["work"].run(0, first)
            elif stage == 1:
                state["work"].run(first, second)
            else:
                state["work"].run(second, size)
                last()

        return run

    def idle(stage):
        if stage == 0:
            hess[...] = jnp.zeros_like(hess)

    for step in range(STEPS):
        used = (step + 1) * RAW
        if SUM_ROWS[step] > used:
            sums[step][used:, :] = jnp.zeros((SUM_ROWS[step] - used, 128), f32)

    pl.semaphore_wait(barrier, n_lat + n_dep - 2)
    copies = send_faces(field_a, 0)

    g = jnp.concatenate([grads_ref[0], grads_ref[1], grads_ref[2], jnp.zeros((64, 64), f32)], axis=0)
    gt = g.T
    gh, gl = split(jnp.concatenate([g, g], axis=1))
    same = (iota((128, 128), 0) < 64) == (iota((128, 128), 1) < 64)
    low_lanes = lane < 64
    none = jnp.zeros((32, 128), f32)
    m_lat = []
    for s in range(2):
        at = slice(s * 16, s * 16 + 16)
        m_lat += [lift_ref[1, at, :], none, lift_ref[0, at, :]]
    place = iota((128, 32), 0) - 4 * iota((128, 32), 1)
    m_dep = dot_exact((place == 3).astype(f32), lift_ref[2]) + dot_exact(
        (place == 0).astype(f32), lift_ref[3]
    )
    mh, ml = split(jnp.concatenate(m_lat + [m_dep], axis=0))
    lift_both[...] = jnp.concatenate([mh, ml], axis=1)

    @pl.loop(0, A_ROWS)
    def _(a):
        for two in range(E_ROWS // 4):
            scaled = []
            for k in range(4):
                row = kappa_ref[a, two * 4 + k : two * 4 + k + 1, :]
                turned = pltpu.roll(row, 64, 1)
                first = jnp.where(low_lanes, row, turned)
                second = jnp.where(low_lanes, turned, row)
                scaled.append(gt * jnp.concatenate([first, first], axis=1))
                scaled.append(gt * jnp.concatenate([second, second], axis=1))
            sh, sl = split(jnp.concatenate(scaled, axis=0))
            blocks = dot3(sh, sl, gh, gl)
            for k in range(4):
                block = jnp.where(same, blocks[k * 128 : (k + 1) * 128], 0.0)
                bh, bl = split(block)
                el = a * E_ROWS + two * 4 + k
                stiff[el] = jnp.concatenate([bh, bl], axis=1)

    operator(field_a, field_b, 0, 1, None, 0, copies)
    copies = send_faces(field_b, 1)
    operator(field_b, field_a, 1, 2, None, 1, copies, lambda: gram(0, 0, 2))
    copies = send_faces(field_a, 0)
    gram(0, 2, 3)
    table = settle(all_sum(0, idle)[:, 0:RAW])
    upper, inverse = eliminate(table)
    receive(copies, 0, 2)
    mix(inverse[2 * NV :], 2, 3, 3)
    shift = jnp.sum(
        jnp.sum(inverse[0:NV, 0:NV] * upper[0:NV, NV : 2 * NV], axis=1, keepdims=True),
        axis=0,
        keepdims=True,
    ) * (1.0 / NV)

    def record_first():
        lower = upper.T
        start[...] = lower[0:NV, 0:NV]
        column0 = dot_exact(inverse[0:NV, 0:NV], lower[NV : 2 * NV, :])
        column1 = dot_exact(
            inverse[NV : 2 * NV, NV : 2 * NV],
            lower[2 * NV :, :] - dot_exact(lower[NV : 2 * NV, 0:NV], column0),
        )
        hess[0:NV, 0:RAW] = column0
        hess[NV : 2 * NV, 0:RAW] = column1
        mix(inverse[0 : 2 * NV, 0 : 2 * NV], 0, 2, 2, False)

    def record(step, prods, tail, inverse):
        known = KNOWN[step]
        base = known * NV
        width = base + RAW
        coefs = jnp.concatenate([prods, tail], axis=1)
        place = iota((NV, width), 1) - iota((NV, width), 0)
        row = CUTS[step]
        hess[row : row + NV, 0:width] = coefs[0:NV] + jnp.where(place == base - NV, shift, 0.0)
        for k in (1, 2):
            at = slice(k * NV, (k + 1) * NV)
            before = slice((k - 1) * NV, k * NV)
            column = coefs[at] + shift * coefs[before]
            reach = base if inverse is None else base + (k - 1) * NV
            column = column - dot_exact(coefs[before, 0:reach], hess[0:reach, 0:width])
            if inverse is not None:
                column = dot_exact(inverse[before, before], column)
            hess[row + k * NV : row + (k + 1) * NV, 0:width] = column

    def images(step, parity, field_last, fill):
        known = KNOWN[step]
        operator(field_a, field_b, known - 1, known, shift)
        copies = send_faces(field_b, parity)
        operator(field_b, field_a, known, known + 1, shift, parity, copies, fill)
        copies = send_faces(field_a, 1 - parity)
        operator(
            field_a, field_last, known + 1, known + 2, shift, 1 - parity, copies, lambda: gram(step, 0, 2)
        )

    images(1, 1, field_b, record_first)
    copies = send_faces(field_b, 1)
    gram(1, 2, 3)
    table = all_sum(1, extend(0))
    prods = table[:, 0 : 3 * NV]
    corner = settle(table[:, 3 * NV : 6 * NV]) - dot_exact(prods, prods, NT)
    upper, inverse = eliminate(corner)
    receive(copies, 1, 5)
    weights = jnp.concatenate([-dot_exact(inverse, prods), inverse], axis=1)
    mix(weights[2 * NV :], 5, 6, 6)

    def record_second():
        record(1, prods, upper.T, inverse)
        mix(weights[0 : 2 * NV, 0 : 5 * NV], 3, 5, 5, False)

    images(2, 0, None, record_second)
    gram(2, 2, 3)
    table = all_sum(2, extend(1))
    prods = table[:, 0 : 6 * NV]
    corner = settle(table[:, 6 * NV : 9 * NV]) - dot_exact(prods, prods, NT)
    record(2, prods, eye(RAW), None)

    spread = hess[CUTS[2] : CUTS[3], 6 * NV : 9 * NV]
    last = extend(2, dot_exact(dot_exact(spread, corner), spread, NT))
    for stage in range(3):
        last(stage)

    answers = [None] * STEPS
    for i in range(STEPS - 1, -1, -1):
        value = ysol[i][...]
        for k in range(i + 1, STEPS):
            value = value - dot_exact(nfac[(k, i)][...].T, answers[k])
        answers[i] = dot_exact(ninv[i][...].T, value)
    solved = jnp.concatenate(answers, axis=0).T
    tail = solved[:, 6 * NV : 8 * NV]
    head = solved[:, 0 : 6 * NV] - dot_exact(tail, prods[0 : 2 * NV, :])
    th, tl = split(jnp.concatenate([head, tail], axis=1))

    @pl.loop(0, A_ROWS)
    def _(a):
        for k in range(0, E_ROWS, 2):
            el = a * E_ROWS + k

            def both(ref):
                return jnp.concatenate([ref[el, 0 : 8 * NV, :], ref[el + 1, 0 : 8 * NV, :]], axis=1)

            value = dot3(th, tl, both(basis_hi), both(basis_lo))
            out_ref[a, k] = value[:, 0:128]
            out_ref[a, k + 1] = value[:, 128:256]


def solution(mesh):
    n_lat, n_dep = mesh.shape["lat"], mesh.shape["dep"]

    def per_device(state, kappa, rate, grads, lift, rhs):
        vmem = pl.BlockSpec(memory_space=pltpu.VMEM)
        V = pltpu.VMEM
        dma = pltpu.SemaphoreType.DMA
        out = pl.pallas_call(
            functools.partial(kernel, n_lat, n_dep),
            out_shape=jax.ShapeDtypeStruct((A_ROWS, E_ROWS, NV, 128), f32),
            in_specs=[vmem] * 6,
            out_specs=vmem,
            scratch_shapes=[
                V((ELEMS + FACES, 9 * NV, 128), bf16),
                V((ELEMS + FACES, 9 * NV, 128), bf16),
                V((ELEMS, 128, 256), bf16),
                V((60, NV, 128), f32),
                V((60, NV, 128), f32),
                V((ELEMS, NV, 128), f32),
                V((64, 128), f32),
                V((ELEMS, 128), f32),
                V((ELEMS, 128), f32),
                V((ELEMS, 128), f32),
                V((ELEMS, 128), f32),
                V((256, 256), bf16),
                V((2, FACES, NV, 128), f32),
                V((2, FACES, NV, 128), f32),
                V((FACES, NV, 128), f32),
                V((256, 384), f32),
                V((NV, NV), f32),
                {
                    (i, k): V((CUTS[i + 1] - CUTS[i], CUTS[k + 1] - CUTS[k]), f32)
                    for i in range(STEPS)
                    for k in range(i)
                },
                [V((CUTS[i + 1] - CUTS[i], CUTS[i + 1] - CUTS[i]), f32) for i in range(STEPS)],
                [V((CUTS[i + 1] - CUTS[i], NV), f32) for i in range(STEPS)],
                [V((rows, 128), f32) for rows in SUM_ROWS],
                [V((n_dep, rows // n_dep, 128), f32) for rows in SUM_ROWS],
                [V((rows // n_dep, 128), f32) for rows in SUM_ROWS],
                [V((n_lat, rows // n_dep, 128), f32) for rows in SUM_ROWS],
                [V((rows, 128), f32) for rows in SUM_ROWS],
                dma((2, 4)),
                dma((2, 4)),
                dma((STEPS, n_dep)),
                dma((STEPS, n_dep)),
                dma((STEPS, n_lat)),
                dma((STEPS, n_lat)),
                dma((STEPS, n_dep)),
                dma((STEPS, n_dep)),
            ],
            compiler_params=pltpu.CompilerParams(
                collective_id=0, has_side_effects=True, vmem_limit_bytes=24 * 1024 * 1024
            ),
        )(
            kappa, state, rate, grads, lift, rhs
        )
        return out

    in_specs = (
        P("lat", "dep", None),
        P("lat", "dep", None),
        P("lat", "dep"),
        P(),
        P(),
        P("lat", "dep", None, None),
    )
    return jax.shard_map(
        per_device, mesh=mesh, in_specs=in_specs, out_specs=P("lat", "dep", None, None), check_vma=False
    )
```

```python
import functools

import jax
import jax.numpy as jnp
from jax import lax
from jax.experimental import pallas as pl
from jax.experimental.pallas import tpu as pltpu
from jax.sharding import PartitionSpec as P

MESH = pl.DeviceIdType.MESH
highest = lax.Precision.HIGHEST
f32 = jnp.float32
bf16 = jnp.bfloat16

A_ROWS, E_ROWS = 4, 8
ELEMS = A_ROWS * E_ROWS
OWN, PAIR, MIX = 32, 32, 8
FACES = 6
NV = 32
STEPS = 3
RAW = 3 * NV
KNOWN = (0, 3, 6)
SUM_ROWS = (128, 192, 320)
CUTS = (0, 64, 160, 256)

NN = (((1,), (0,)), ((), ()))
NT = (((1,), (1,)), ((), ()))


def split(x):
    hi = x.astype(bf16)
    return hi, (x - hi.astype(f32)).astype(bf16)


def dot(a, b, dims=NN):
    return lax.dot_general(a, b, dims, preferred_element_type=f32)


def dot_exact(a, b, dims=NN):
    return lax.dot_general(a, b, dims, precision=highest, preferred_element_type=f32)


def dot3(ah, al, bh, bl, dims=NN):
    rows = ah.shape[0]
    both = dot(jnp.concatenate([ah, al], axis=0), bh, dims)
    return both[:rows] + both[rows:] + dot(ah, bl, dims)


def dot_wide(ah, al, both):
    first = dot(ah, both)
    return first[:, 0:128] + (first[:, 128:256] + dot(al, both[:, 0:128]))


def dot4(ah, al, bh, bl, dims=NN):
    rows = ah.shape[0]
    stacked = jnp.concatenate([ah, al], axis=0)
    high = dot(stacked, bh, dims)
    low = dot(stacked, bl, dims)
    return high[:rows] + (high[rows:] + (low[:rows] + low[rows:]))


def iota(shape, dim):
    return lax.broadcasted_iota(jnp.int32, shape, dim)


def eye(n):
    return (iota((n, n), 0) == iota((n, n), 1)).astype(f32)


class Elimination:
    def __init__(self, gram):
        self.n = gram.shape[0]
        wide = jnp.concatenate([gram, eye(self.n)], axis=1)
        self.tiles = [wide[8 * i : 8 * i + 8] for i in range(self.n // 8)]

    def run(self, begin, end):
        width = 2 * self.n
        row = iota((8, width), 0)

        def column(x, k):
            return jnp.broadcast_to(x[:, k : k + 1], (8, width))

        for k in range(begin, end, 4):
            p, q = k // 8, k % 8
            x = self.tiles[p]
            head = [column(x, k + j) for j in range(4)]
            row0, row1, row2, row3 = (x[q + j : q + j + 1, :] for j in range(4))
            a, b, c = head[0][q : q + 1], head[1][q : q + 1], head[1][q + 1 : q + 2]
            a_inv = 1.0 / a
            t = b * a_inv
            d_inv = a * (1.0 / (a * c - b * b))
            scaled0 = row0 * a_inv
            scaled1 = (row1 - t * row0) * d_inv
            f02, f03 = head[2][q : q + 1] * a_inv, head[3][q : q + 1] * a_inv
            f12 = (head[2][q + 1 : q + 2] - t * head[2][q : q + 1]) * d_inv
            f13 = (head[3][q + 1 : q + 2] - t * head[3][q : q + 1]) * d_inv

            def reduced(columns):
                c0, c1, c2, c3 = columns
                c1 = c1 - c0 * t
                return c0, c1, c2 - c0 * f02 - c1 * f12, c3 - c0 * f03 - c1 * f13

            h0, h1, h2, h3 = reduced(head)
            row2 = row2 - h0[q + 2 : q + 3] * scaled0 - h1[q + 2 : q + 3] * scaled1
            row3 = row3 - h0[q + 3 : q + 4] * scaled0 - h1[q + 3 : q + 4] * scaled1
            a, b, c = h2[q + 2 : q + 3], h3[q + 2 : q + 3], h3[q + 3 : q + 4]
            a_inv = 1.0 / a
            t2 = b * a_inv
            d_inv = a * (1.0 / (a * c - b * b))
            scaled2 = row2 * a_inv
            scaled3 = (row3 - t2 * row2) * d_inv
            for i in range(p, self.n // 8):
                x = self.tiles[i]
                if i == p:
                    c0, c1, c2, c3 = h0, h1, h2, h3 - h2 * t2
                    c0 = jnp.where(row > q, c0, 0.0)
                    c1 = jnp.where(row > q + 1, c1, 0.0)
                    c2 = jnp.where(row > q + 2, c2, 0.0)
                    c3 = jnp.where(row > q + 3, c3, 0.0)
                else:
                    c0, c1, c2, c3 = reduced([column(x, k + j) for j in range(4)])
                    c3 = c3 - c2 * t2
                self.tiles[i] = x - c0 * scaled0 - c1 * scaled1 - c2 * scaled2 - c3 * scaled3

    def finish(self):
        n, width = self.n, 2 * self.n
        wide = jnp.concatenate(self.tiles, axis=0)
        on_diag = iota((n, width), 0) == iota((n, width), 1)
        pivots = jnp.sum(jnp.where(on_diag, wide, 0.0), axis=1, keepdims=True)
        wide = wide * lax.rsqrt(pivots)
        upper = jnp.where(iota((n, n), 0) <= iota((n, n), 1), wide[:, :n], 0.0)
        return upper, wide[:, n:]


def eliminate(gram):
    work = Elimination(gram)
    work.run(0, work.n)
    return work.finish()


def kernel(
    n_lat,
    n_dep,
    kappa_hbm,
    state_hbm,
    rate_hbm,
    grads_hbm,
    lift_hbm,
    rhs_hbm,
    out_ref,
    kappa_ref,
    state_ref,
    rate_ref,
    grads_ref,
    lift_ref,
    rhs_ref,
    fetch_sem,
    basis_hi,
    basis_lo,
    stiff,
    field_a,
    field_b,
    own,
    kappa_pad,
    kappa_x,
    kappa_z,
    diag,
    cross,
    lift_both,
    halo_out,
    halo_in,
    halo_mix,
    hess,
    start,
    nfac,
    ninv,
    ysol,
    sums,
    take_a,
    part,
    take_b,
    total,
    halo_send,
    halo_recv,
    a_send,
    a_recv,
    b_send,
    b_recv,
    c_send,
    c_recv,
):
    lat = lax.axis_index("lat")
    dep = lax.axis_index("dep")

    fetches = []
    for index, (source, target) in enumerate(
        (
            (rhs_hbm, rhs_ref),
            (kappa_hbm, kappa_ref),
            (state_hbm, state_ref),
            (rate_hbm, rate_ref),
            (grads_hbm, grads_ref),
            (lift_hbm, lift_ref),
        )
    ):
        fetches.append(pltpu.make_async_copy(source, target, fetch_sem.at[index]))
        fetches[-1].start()

    barrier = pltpu.get_barrier_semaphore()
    for k in range(1, n_dep):
        pl.semaphore_signal(
            barrier, inc=1, device_id=(lat, lax.rem(dep + k, n_dep)), device_id_type=MESH
        )
    for k in range(1, n_lat):
        pl.semaphore_signal(
            barrier, inc=1, device_id=(lax.rem(lat + k, n_lat), dep), device_id_type=MESH
        )

    lane = iota((1, 128), 1)
    node_x = lane % 64 // 16
    node_z = lane % 4

    def padded(el):
        return (el // E_ROWS + 1) * 10 + el % E_ROWS + 1

    for fetch in fetches:
        fetch.wait()

    touches = (node_x == 0) | (node_x == 3)
    touches = touches.astype(f32) + ((node_z == 0) | (node_z == 3)).astype(f32)
    kappa_pad[...] = jnp.ones_like(kappa_pad)
    for a in range(A_ROWS):
        here = slice(a * E_ROWS, (a + 1) * E_ROWS)
        kappa = kappa_ref[a]
        picked = iota((E_ROWS, E_ROWS), 0) == iota((E_ROWS, E_ROWS), 1)
        speed = jnp.sum(jnp.where(picked, rate_ref[a : a + 1, :], 0.0), axis=1, keepdims=True)
        diag[here, :] = 0.25 + kappa * touches
        cross[here, :] = speed * pltpu.roll(state_ref[a], 64, 1)
        kappa_x[here, :] = pltpu.roll(kappa, 80, 1)
        kappa_z[here, :] = pltpu.roll(kappa, 125, 1)
        base = (a + 1) * 10 + 1
        kappa_pad[base : base + E_ROWS, :] = kappa
        for side in (0, E_ROWS + 1):
            field_a[(a + 1) * 10 + side] = jnp.zeros((NV, 128), f32)
            field_b[(a + 1) * 10 + side] = jnp.zeros((NV, 128), f32)

    for p in (4, 5):
        for ref in (basis_hi, basis_lo):
            ref[ELEMS + p, 0 : 6 * NV, :] = jnp.zeros((6 * NV, 128), bf16)
    for a in range(A_ROWS):
        for e in range(E_ROWS):
            el = a * E_ROWS + e
            v = rhs_ref[a, e]
            vh, vl = split(v)
            basis_hi[el, 0:NV, :] = vh
            basis_lo[el, 0:NV, :] = vl
            field_a[padded(el)] = v

    def halo_copies(slot):
        right, left = lax.rem(lat + 1, n_lat), lax.rem(lat + n_lat - 1, n_lat)
        copies = []
        for index, (start, size, where) in enumerate(
            (
                (0, 2, (right, dep)),
                (2, 2, (left, dep)),
                (4, 1, (lat, lax.rem(dep + 1, n_dep))),
                (5, 1, (lat, lax.rem(dep + n_dep - 1, n_dep))),
            )
        ):
            copies.append(
                pltpu.make_async_remote_copy(
                    src_ref=halo_out.at[slot, pl.ds(start, size)],
                    dst_ref=halo_in.at[slot, pl.ds(start, size)],
                    send_sem=halo_send.at[slot, index],
                    recv_sem=halo_recv.at[slot, index],
                    device_id=where,
                    device_id_type=MESH,
                )
            )
        return copies

    has_above = dep < n_dep - 1
    has_below = dep > 0

    def send_faces(field, parity):
        for p in range(2):
            right = None
            left = None
            for k in range(4):
                e = 4 * p + k
                index = 4 * 10 + e + 1
                there = pltpu.roll(
                    field[index] * kappa_pad[index : index + 1, :], (80 + 16 * k) % 128, 1
                )
                back = pltpu.roll(field[10 + e + 1], 16 * k, 1)
                mask = node_x == k
                right = there if right is None else jnp.where(mask, there, right)
                left = back if left is None else jnp.where(mask, back, left)
            halo_out[parity, p] = right
            halo_out[parity, 2 + p] = left
        up = None
        down = None
        for k in range(A_ROWS):
            index = (k + 1) * 10 + E_ROWS
            there = pltpu.roll(
                field[index] * kappa_pad[index : index + 1, :], (125 + k) % 128, 1
            )
            back = pltpu.roll(field[(k + 1) * 10 + 1], k, 1)
            mask = node_z == k
            up = there if up is None else jnp.where(mask, there, up)
            down = back if down is None else jnp.where(mask, back, down)
        halo_out[parity, 4] = up
        halo_out[parity, 5] = down
        copies = halo_copies(parity)
        copies[0].start()
        copies[1].start()

        @pl.when(has_above)
        def _():
            copies[2].start()

        @pl.when(has_below)
        def _():
            copies[3].start()

        return copies

    def receive(copies, parity, slot):
        def keep(p):
            if slot < 6:
                fh, fl = split(halo_in[parity, p])
                basis_hi[ELEMS + p, slot * NV : (slot + 1) * NV, :] = fh
                basis_lo[ELEMS + p, slot * NV : (slot + 1) * NV, :] = fl

        copies[0].wait()
        copies[1].wait()
        for p in range(4):
            keep(p)

        @pl.when(has_above)
        def _():
            copies[2].wait_send()
            copies[3].wait_recv()
            keep(5)

        @pl.when(has_below)
        def _():
            copies[3].wait_send()
            copies[2].wait_recv()
            keep(4)

    def unpack(field, faces):
        for p in range(2):
            for k in range(4):
                e = 4 * p + k
                field[e + 1] = pltpu.roll(faces[p], (48 - 16 * k) % 128, 1)
                field[5 * 10 + e + 1] = pltpu.roll(faces[2 + p], (128 - 16 * k) % 128, 1)

        @pl.when(has_below)
        def _():
            for k in range(A_ROWS):
                field[(k + 1) * 10] = pltpu.roll(faces[4], 3 - k, 1)

        @pl.when(has_above)
        def _():
            for k in range(A_ROWS):
                field[(k + 1) * 10 + E_ROWS + 1] = pltpu.roll(faces[5], (128 - k) % 128, 1)

    def operator(field, field_out, slot_in, slot_out, shift, parity=0, copies=None, fill=lambda: None):
        @pl.loop(0, ELEMS // OWN)
        def _(group):
            for k in range(OWN):
                el = group * OWN + k
                xh = basis_hi[el, slot_in * NV : (slot_in + 1) * NV, :]
                xl = basis_lo[el, slot_in * NV : (slot_in + 1) * NV, :]
                x = field[padded(el)]
                z = x * cross[pl.ds(el, 1), :]
                y = dot_wide(xh, xl, stiff[el])
                here = diag[pl.ds(el, 1), :]
                if shift is not None:
                    here = here - shift
                own[el] = y + x * here + (z + pltpu.roll(z, 64, 1))

        if copies is None:
            unpack(field, halo_mix)
        else:
            fill()
            receive(copies, parity, slot_in)
            unpack(field, halo_in.at[parity])

        @pl.loop(0, ELEMS // PAIR)
        def _(bunch):
            for part_of in range(PAIR // 4):
                vectors = []
                for k in range(4):
                    el = bunch * PAIR + part_of * 4 + k
                    at = padded(el)
                    sideways = jnp.where(
                        node_x == 3,
                        kappa_pad[pl.ds(at - 10, 1), :] * field[at - 10],
                        kappa_x[pl.ds(el, 1), :] * field[at + 10],
                    )
                    upright = jnp.where(
                        node_z == 3,
                        kappa_pad[pl.ds(at - 1, 1), :] * field[at - 1],
                        kappa_z[pl.ds(el, 1), :] * field[at + 1],
                    )
                    vectors.append(jnp.concatenate([sideways, upright], axis=1))
                ch, cl = split(jnp.concatenate(vectors, axis=0))
                coupled = dot_wide(ch, cl, lift_both[...])
                for k in range(4):
                    el = bunch * PAIR + part_of * 4 + k
                    w = own[el] - coupled[k * NV : (k + 1) * NV]
                    wh, wl = split(w)
                    basis_hi[el, slot_out * NV : (slot_out + 1) * NV, :] = wh
                    basis_lo[el, slot_out * NV : (slot_out + 1) * NV, :] = wl
                    if field_out is not None:
                        field_out[padded(el)] = w

    def gram(step, begin, end):
        known = KNOWN[step] * NV
        first, stop = known + begin * NV, known + end * NV
        rows = slice(begin * NV, end * NV)

        def body(octet, acc):
            def wide(ref, lower, upper):
                return jnp.concatenate([ref[octet * 8 + k, lower:upper, :] for k in range(8)], axis=1)

            wh, wl = wide(basis_hi, first, stop), wide(basis_lo, first, stop)
            bh, bl = wide(basis_hi, 0, stop), wide(basis_lo, 0, stop)
            return acc + dot4(wh, wl, bh, bl, NT)

        value = lax.fori_loop(0, ELEMS // 8, body, jnp.zeros((stop - first, stop), f32))
        for i in range(step + 1):
            filled = max(0, min(128, stop - i * 128))
            parts = [value[:, i * 128 : i * 128 + filled]] if filled else []
            if filled < 128:
                parts.append(jnp.zeros((stop - first, 128 - filled), f32))
            piece = jnp.concatenate(parts, axis=1) if len(parts) > 1 else parts[0]
            sums[step][i * RAW + begin * NV : i * RAW + end * NV, :] = piece

    def settle(table):
        upper = (iota((RAW, RAW), 0) < 2 * NV) & (iota((RAW, RAW), 1) >= 2 * NV)
        return jnp.where(upper, table.T, table)

    def all_sum(step, work):
        size = SUM_ROWS[step] // n_dep
        mine = pl.ds(pl.multiple_of(dep * size, 8), size)
        copies_a = []
        for k in range(1, n_dep):
            to = lax.rem(dep + k, n_dep)
            copies_a.append(
                pltpu.make_async_remote_copy(
                    src_ref=sums[step].at[pl.ds(pl.multiple_of(to * size, 8), size)],
                    dst_ref=take_a[step].at[k],
                    send_sem=a_send.at[step, k],
                    recv_sem=a_recv.at[step, k],
                    device_id=(lat, to),
                    device_id_type=MESH,
                )
            )
            copies_a[-1].start()
        work(0)
        value = sums[step][mine, :]
        for k in range(1, n_dep):
            copies_a[k - 1].wait_recv()
            value = value + take_a[step][k]
        part[step][...] = value
        copies_b = []
        for k in range(1, n_lat):
            copies_b.append(
                pltpu.make_async_remote_copy(
                    src_ref=part[step],
                    dst_ref=take_b[step].at[lat],
                    send_sem=b_send.at[step, k],
                    recv_sem=b_recv.at[step, k],
                    device_id=(lax.rem(lat + k, n_lat), dep),
                    device_id_type=MESH,
                )
            )
            copies_b[-1].start()
        take_b[step][lat] = value
        work(1)
        for copy in copies_b:
            copy.wait_recv()
        value = take_b[step][0]
        for k in range(1, n_lat):
            value = value + take_b[step][k]
        total[step][mine, :] = value
        copies_c = []
        for k in range(1, n_dep):
            copies_c.append(
                pltpu.make_async_remote_copy(
                    src_ref=total[step].at[mine],
                    dst_ref=total[step].at[mine],
                    send_sem=c_send.at[step, k],
                    recv_sem=c_recv.at[step, k],
                    device_id=(lat, lax.rem(dep + k, n_dep)),
                    device_id_type=MESH,
                )
            )
            copies_c[-1].start()
        work(2)
        for copy in copies_c:
            copy.wait_recv()
        for copy in copies_a + copies_b + copies_c:
            copy.wait_send()
        return jnp.concatenate(
            [total[step][i * RAW : (i + 1) * RAW, :] for i in range(step + 1)], axis=1
        )

    def mix(table, first, stop, reach, to_field=True):
        th, tl = split(table)

        def two(el, ghost):
            def both(ref):
                return jnp.concatenate(
                    [ref[el, 0 : reach * NV, :], ref[el + 1, 0 : reach * NV, :]], axis=1
                )

            fresh = dot3(th, tl, both(basis_hi), both(basis_lo))
            fh, fl = split(fresh)
            for half in range(2):
                cut = slice(half * 128, half * 128 + 128)
                basis_hi[el + half, first * NV : stop * NV, :] = fh[:, cut]
                basis_lo[el + half, first * NV : stop * NV, :] = fl[:, cut]
                if to_field and ghost:
                    halo_mix[el + half - ELEMS] = fresh[:, cut]
                elif to_field:
                    field_a[padded(el + half)] = fresh[:, cut]

        @pl.loop(0, ELEMS // MIX)
        def _(bunch):
            for k in range(0, MIX, 2):
                two(bunch * MIX + k, False)

        for p in range(0, FACES, 2):
            two(ELEMS + p, True)

    def extend(step, metric=None):
        begin, end = CUTS[step], CUTS[step + 1]
        size = end - begin
        state = {}

        def products():
            new = hess[begin:end, :]
            if metric is None:
                rows = dot_exact(new, hess[0:end, :], NT)
            else:
                rows = dot_exact(new[:, 0:192], hess[0:end, 0:192], NT)
            right = dot_exact(new[:, 0:NV], start[...], NT)
            corner = rows[:, begin:end]
            if metric is not None:
                corner = corner + metric
            pieces = []
            for i in range(step):
                block = rows[:, CUTS[i] : CUTS[i + 1]]
                for k in range(i):
                    block = block - dot_exact(pieces[k], nfac[(i, k)][...], NT)
                block = dot_exact(block, ninv[i][...], NT)
                pieces.append(block)
                nfac[(step, i)][...] = block
                right = right - dot_exact(block, ysol[i][...])
            for block in pieces:
                corner = corner - dot_exact(block, block, NT)
            state["right"] = right
            state["work"] = Elimination(corner)

        def last():
            _, inverse = state["work"].finish()
            ninv[step][...] = inverse
            ysol[step][...] = dot_exact(inverse, state["right"])

        def run(stage):
            first, second = size // 4 // 4 * 4, size * 3 // 4 // 4 * 4
            if stage == 0:
                products()
                state["work"].run(0, first)
            elif stage == 1:
                state["work"].run(first, second)
            else:
                state["work"].run(second, size)
                last()

        return run

    def idle(stage):
        if stage == 0:
            hess[...] = jnp.zeros_like(hess)

    for step in range(STEPS):
        used = (step + 1) * RAW
        if SUM_ROWS[step] > used:
            sums[step][used:, :] = jnp.zeros((SUM_ROWS[step] - used, 128), f32)

    pl.semaphore_wait(barrier, n_lat + n_dep - 2)
    copies = send_faces(field_a, 0)

    g = jnp.concatenate([grads_ref[0], grads_ref[1], grads_ref[2], jnp.zeros((64, 64), f32)], axis=0)
    gt = g.T
    gh, gl = split(jnp.concatenate([g, g], axis=1))
    same = (iota((128, 128), 0) < 64) == (iota((128, 128), 1) < 64)
    low_lanes = lane < 64
    none = jnp.zeros((32, 128), f32)
    m_lat = []
    for s in range(2):
        at = slice(s * 16, s * 16 + 16)
        m_lat += [lift_ref[1, at, :], none, lift_ref[0, at, :]]
    place = iota((128, 32), 0) - 4 * iota((128, 32), 1)
    m_dep = dot_exact((place == 3).astype(f32), lift_ref[2]) + dot_exact(
        (place == 0).astype(f32), lift_ref[3]
    )
    mh, ml = split(jnp.concatenate(m_lat + [m_dep], axis=0))
    lift_both[...] = jnp.concatenate([mh, ml], axis=1)

    @pl.loop(0, A_ROWS)
    def _(a):
        for two in range(E_ROWS // 4):
            scaled = []
            for k in range(4):
                row = kappa_ref[a, two * 4 + k : two * 4 + k + 1, :]
                turned = pltpu.roll(row, 64, 1)
                first = jnp.where(low_lanes, row, turned)
                second = jnp.where(low_lanes, turned, row)
                scaled.append(gt * jnp.concatenate([first, first], axis=1))
                scaled.append(gt * jnp.concatenate([second, second], axis=1))
            sh, sl = split(jnp.concatenate(scaled, axis=0))
            blocks = dot3(sh, sl, gh, gl)
            for k in range(4):
                block = jnp.where(same, blocks[k * 128 : (k + 1) * 128], 0.0)
                bh, bl = split(block)
                el = a * E_ROWS + two * 4 + k
                stiff[el] = jnp.concatenate([bh, bl], axis=1)

    operator(field_a, field_b, 0, 1, None, 0, copies)
    copies = send_faces(field_b, 1)
    operator(field_b, field_a, 1, 2, None, 1, copies, lambda: gram(0, 0, 2))
    copies = send_faces(field_a, 0)
    gram(0, 2, 3)
    table = settle(all_sum(0, idle)[:, 0:RAW])
    upper, inverse = eliminate(table)
    receive(copies, 0, 2)
    mix(inverse[2 * NV :], 2, 3, 3)
    shift = jnp.sum(
        jnp.sum(inverse[0:NV, 0:NV] * upper[0:NV, NV : 2 * NV], axis=1, keepdims=True),
        axis=0,
        keepdims=True,
    ) * (1.0 / NV)

    def record_first():
        lower = upper.T
        start[...] = lower[0:NV, 0:NV]
        column0 = dot_exact(inverse[0:NV, 0:NV], lower[NV : 2 * NV, :])
        column1 = dot_exact(
            inverse[NV : 2 * NV, NV : 2 * NV],
            lower[2 * NV :, :] - dot_exact(lower[NV : 2 * NV, 0:NV], column0),
        )
        hess[0:NV, 0:RAW] = column0
        hess[NV : 2 * NV, 0:RAW] = column1
        mix(inverse[0 : 2 * NV, 0 : 2 * NV], 0, 2, 2, False)

    def record(step, prods, tail, inverse):
        known = KNOWN[step]
        base = known * NV
        width = base + RAW
        coefs = jnp.concatenate([prods, tail], axis=1)
        place = iota((NV, width), 1) - iota((NV, width), 0)
        row = CUTS[step]
        hess[row : row + NV, 0:width] = coefs[0:NV] + jnp.where(place == base - NV, shift, 0.0)
        for k in (1, 2):
            at = slice(k * NV, (k + 1) * NV)
            before = slice((k - 1) * NV, k * NV)
            column = coefs[at] + shift * coefs[before]
            reach = base if inverse is None else base + (k - 1) * NV
            column = column - dot_exact(coefs[before, 0:reach], hess[0:reach, 0:width])
            if inverse is not None:
                column = dot_exact(inverse[before, before], column)
            hess[row + k * NV : row + (k + 1) * NV, 0:width] = column

    def images(step, parity, field_last, fill):
        known = KNOWN[step]
        operator(field_a, field_b, known - 1, known, shift)
        copies = send_faces(field_b, parity)
        operator(field_b, field_a, known, known + 1, shift, parity, copies, fill)
        copies = send_faces(field_a, 1 - parity)
        operator(
            field_a, field_last, known + 1, known + 2, shift, 1 - parity, copies, lambda: gram(step, 0, 2)
        )

    images(1, 1, field_b, record_first)
    copies = send_faces(field_b, 1)
    gram(1, 2, 3)
    table = all_sum(1, extend(0))
    prods = table[:, 0 : 3 * NV]
    corner = settle(table[:, 3 * NV : 6 * NV]) - dot_exact(prods, prods, NT)
    upper, inverse = eliminate(corner)
    receive(copies, 1, 5)
    weights = jnp.concatenate([-dot_exact(inverse, prods), inverse], axis=1)
    mix(weights[2 * NV :], 5, 6, 6)

    def record_second():
        record(1, prods, upper.T, inverse)
        mix(weights[0 : 2 * NV, 0 : 5 * NV], 3, 5, 5, False)

    images(2, 0, None, record_second)
    gram(2, 2, 3)
    table = all_sum(2, extend(1))
    prods = table[:, 0 : 6 * NV]
    corner = settle(table[:, 6 * NV : 9 * NV]) - dot_exact(prods, prods, NT)
    record(2, prods, eye(RAW), None)

    spread = hess[CUTS[2] : CUTS[3], 6 * NV : 9 * NV]
    last = extend(2, dot_exact(dot_exact(spread, corner), spread, NT))
    for stage in range(3):
        last(stage)

    answers = [None] * STEPS
    for i in range(STEPS - 1, -1, -1):
        value = ysol[i][...]
        for k in range(i + 1, STEPS):
            value = value - dot_exact(nfac[(k, i)][...].T, answers[k])
        answers[i] = dot_exact(ninv[i][...].T, value)
    solved = jnp.concatenate(answers, axis=0).T
    tail = solved[:, 6 * NV : 8 * NV]
    head = solved[:, 0 : 6 * NV] - dot_exact(tail, prods[0 : 2 * NV, :])
    th, tl = split(jnp.concatenate([head, tail], axis=1))

    @pl.loop(0, A_ROWS)
    def _(a):
        for k in range(0, E_ROWS, 2):
            el = a * E_ROWS + k

            def both(ref):
                return jnp.concatenate([ref[el, 0 : 8 * NV, :], ref[el + 1, 0 : 8 * NV, :]], axis=1)

            value = dot3(th, tl, both(basis_hi), both(basis_lo))
            out_ref[a, k] = value[:, 0:128]
            out_ref[a, k + 1] = value[:, 128:256]


def solution(mesh):
    n_lat, n_dep = mesh.shape["lat"], mesh.shape["dep"]

    def per_device(state, kappa, rate, grads, lift, rhs):
        vmem = pl.BlockSpec(memory_space=pltpu.VMEM)
        V = pltpu.VMEM
        dma = pltpu.SemaphoreType.DMA
        out = pl.pallas_call(
            functools.partial(kernel, n_lat, n_dep),
            out_shape=jax.ShapeDtypeStruct((A_ROWS, E_ROWS, NV, 128), f32),
            in_specs=[pl.BlockSpec(memory_space=pltpu.HBM)] * 6,
            out_specs=vmem,
            scratch_shapes=[
                V(kappa.shape, f32),
                V(state.shape, f32),
                V(rate.shape, f32),
                V(grads.shape, f32),
                V(lift.shape, f32),
                V(rhs.shape, f32),
                dma((6,)),
                V((ELEMS + FACES, 9 * NV, 128), bf16),
                V((ELEMS + FACES, 9 * NV, 128), bf16),
                V((ELEMS, 128, 256), bf16),
                V((60, NV, 128), f32),
                V((60, NV, 128), f32),
                V((ELEMS, NV, 128), f32),
                V((64, 128), f32),
                V((ELEMS, 128), f32),
                V((ELEMS, 128), f32),
                V((ELEMS, 128), f32),
                V((ELEMS, 128), f32),
                V((256, 256), bf16),
                V((2, FACES, NV, 128), f32),
                V((2, FACES, NV, 128), f32),
                V((FACES, NV, 128), f32),
                V((256, 384), f32),
                V((NV, NV), f32),
                {
                    (i, k): V((CUTS[i + 1] - CUTS[i], CUTS[k + 1] - CUTS[k]), f32)
                    for i in range(STEPS)
                    for k in range(i)
                },
                [V((CUTS[i + 1] - CUTS[i], CUTS[i + 1] - CUTS[i]), f32) for i in range(STEPS)],
                [V((CUTS[i + 1] - CUTS[i], NV), f32) for i in range(STEPS)],
                [V((rows, 128), f32) for rows in SUM_ROWS],
                [V((n_dep, rows // n_dep, 128), f32) for rows in SUM_ROWS],
                [V((rows // n_dep, 128), f32) for rows in SUM_ROWS],
                [V((n_lat, rows // n_dep, 128), f32) for rows in SUM_ROWS],
                [V((rows, 128), f32) for rows in SUM_ROWS],
                dma((2, 4)),
                dma((2, 4)),
                dma((STEPS, n_dep)),
                dma((STEPS, n_dep)),
                dma((STEPS, n_lat)),
                dma((STEPS, n_lat)),
                dma((STEPS, n_dep)),
                dma((STEPS, n_dep)),
            ],
            compiler_params=pltpu.CompilerParams(
                collective_id=0, has_side_effects=True, vmem_limit_bytes=60 * 1024 * 1024
            ),
        )(
            kappa, state, rate, grads, lift, rhs
        )
        return out

    in_specs = (
        P("lat", "dep", None),
        P("lat", "dep", None),
        P("lat", "dep"),
        P(),
        P(),
        P("lat", "dep", None, None),
    )
    return jax.shard_map(
        per_device, mesh=mesh, in_specs=in_specs, out_specs=P("lat", "dep", None, None), check_vma=False
    )
```
